32 devices in a mesh: tm: 16 (over z, y, x), tile: 2 (over core).
Axes of the slice: x: 2, y: 2, z: 4, core: 2. Of those that a mesh axis runs over, the one named last changes fastest.
Arguments:
- latent: bfloat16 [64, 8, 160, 128], P('tm', 'tile'), may hold values from -6 to 6
- cot_forward: bfloat16 [64, 8, 160, 128], P('tm', 'tile'), may hold values from -6 to 6
- cot_reverse: bfloat16 [64, 8, 160, 128], P('tm', 'tile'), may hold values from -6 to 6
- spatial_weight: bfloat16 [3, 3, 128, 128], replicated, may hold values from -0.1875 to 0.1875
- temporal_weight: bfloat16 [3, 128, 128], replicated, may hold values from -0.3125 to 0.3125
Outputs:
- out_forward: bfloat16 [64, 8, 160, 128], P('tm', 'tile')
- out_reverse: bfloat16 [64, 8, 160, 128], P('tm', 'tile')
- grad_input: bfloat16 [64, 8, 160, 128], P('tm', 'tile')
- grad_spatial: float32 [3, 3, 128, 128], replicated
- grad_temporal: float32 [3, 128, 128], replicated
The draws below stay inside these ranges and needn't reach their ends.
All inputs are finite; a program needn't handle non-finite values.
Results may differ from the reference program's by a relative error of at most 0.0032.
Values may be sent and summed in bfloat16 or wider, within the bound.
A program may use at most 64 MiB of HBM per device.

```python
import math
import jax
import jax.numpy as jnp
from jax import lax

C = 128
W = 160
FRAMES = 64
ROWS = 8


def levels(key, extent, pieces, least, largest):
    factor_of, own = 1.0, jax.random.fold_in(key, 6)
    for axis_at, blocks in pieces:
        steps = jnp.exp(jax.random.uniform(jax.random.fold_in(own, axis_at), (blocks,), jnp.float32, least / len(pieces), largest / len(pieces)))
        factor_of = factor_of * jnp.repeat(steps, extent[axis_at] // blocks).reshape([-1 if axis == axis_at else 1 for axis in range(len(extent))])
    return factor_of


def noise(stream_key, extent, spread, reach, pieces=(), kind=jnp.bfloat16):
    drawn = jax.random.normal(stream_key, extent, jnp.float32) * spread
    if len(pieces) > 0:
        drawn = levels(stream_key, extent, pieces, -0.22, 0.18) * drawn
    return jnp.clip(drawn, min=-reach, max=reach).astype(kind)


def setup_inputs(seed: int = 0) -> dict:
    splits = jax.random.split(jax.random.key(seed), 6)
    latent = noise(splits[0], (FRAMES, ROWS, W, C), 1.0, 6.0, ((0, 16), (1, 2)))
    cot_forward = noise(splits[1], (FRAMES, ROWS, W, C), 1.0, 6.0, ((0, 16), (1, 2)))
    cot_reverse = noise(splits[2], (FRAMES, ROWS, W, C), 1.0, 6.0, ((0, 16), (1, 2)))
    spatial_weight = noise(splits[3], (3, 3, C, C), (9 * C) ** -0.5, 0.1875)
    temporal_weight = noise(splits[4], (3, C, C), (3 * C) ** -0.5, 0.3125)
    return {"latent": latent, "cot_forward": cot_forward, "cot_reverse": cot_reverse, "spatial_weight": spatial_weight, "temporal_weight": temporal_weight}


def flat(values):
    return values.reshape(-1, values.shape[-1])

def shift_frames(values, lag_steps):
    if lag_steps > 0:
        return jnp.concatenate([jnp.zeros_like(values[:lag_steps]), values[:-lag_steps]], axis=0)
    if lag_steps < 0:
        return jnp.concatenate([values[-lag_steps:], jnp.zeros_like(values[:-lag_steps])], axis=0)
    return values

def contract_rows(left, right):
    return lax.dot_general(left, right, (((0,), (0,)), ((), ())), preferred_element_type=jnp.float32)

def reference(latent, cot_forward, cot_reverse, spatial_weight, temporal_weight):
    frame_count, height, width_cells, channels = latent.shape
    padded = jnp.pad(latent, ((0, 0), (1, 1), (1, 1), (0, 0)))
    pre_act = jnp.zeros((frame_count * height * width_cells, channels), jnp.float32)
    for row_step in range(3):
        for col_step in range(3):
            window = flat(padded[:, row_step:row_step + height, col_step:col_step + width_cells, :])
            pre_act = pre_act + jnp.dot(window, spatial_weight[row_step, col_step], preferred_element_type=jnp.float32)
    act = jax.nn.silu(pre_act).astype(jnp.bfloat16).reshape(latent.shape)

    def causal_out(source_latent, source_act):
        total = flat(source_latent).astype(jnp.float32)
        for lag_steps in range(3):
            total = total + jnp.dot(flat(shift_frames(source_act, lag_steps)), temporal_weight[lag_steps], preferred_element_type=jnp.float32)
        return total.astype(jnp.bfloat16).reshape(latent.shape)
    out_forward = causal_out(latent, act)
    out_reverse = causal_out(latent[::-1], act[::-1])[::-1]
    grad_act = jnp.zeros((frame_count * height * width_cells, channels), jnp.float32)
    grad_temp = []
    for lag_steps in range(3):
        weight_back = jnp.transpose(temporal_weight[lag_steps])
        grad_act = grad_act + jnp.dot(flat(shift_frames(cot_forward, -lag_steps)), weight_back, preferred_element_type=jnp.float32)
        grad_act = grad_act + jnp.dot(flat(shift_frames(cot_reverse, lag_steps)), weight_back, preferred_element_type=jnp.float32)
        term = contract_rows(flat(shift_frames(act, lag_steps)), flat(cot_forward))
        term = term + contract_rows(flat(shift_frames(act, -lag_steps)), flat(cot_reverse))
        grad_temp.append(term)
    sigmoid_pre = jax.nn.sigmoid(pre_act)
    grad_pre = (grad_act * sigmoid_pre * (1.0 + pre_act * (1.0 - sigmoid_pre))).astype(jnp.bfloat16)
    grad_padded = jnp.pad(grad_pre.reshape(latent.shape), ((0, 0), (1, 1), (1, 1), (0, 0)))
    total_in = flat(cot_forward).astype(jnp.float32) + flat(cot_reverse).astype(jnp.float32)
    grad_space = []
    for row_step in range(3):
        for col_step in range(3):
            window = flat(grad_padded[:, 2 - row_step:2 - row_step + height, 2 - col_step:2 - col_step + width_cells, :])
            total_in = total_in + jnp.dot(window, jnp.transpose(spatial_weight[row_step, col_step]), preferred_element_type=jnp.float32)
            source = flat(padded[:, row_step:row_step + height, col_step:col_step + width_cells, :])
            grad_space.append(contract_rows(source, grad_pre))
    grad_input = total_in.astype(jnp.bfloat16).reshape(latent.shape)
    grad_scale = 1.0 / math.sqrt(frame_count * height * width_cells)
    grad_spatial = jnp.stack(grad_space).reshape(3, 3, channels, channels) * grad_scale
    grad_temporal = jnp.stack(grad_temp) * grad_scale
    return (out_forward, out_reverse, grad_input, grad_spatial, grad_temporal)
```

```python
import functools
import math

import jax
import jax.numpy as jnp
from jax import lax
from jax.experimental import pallas as pl
from jax.experimental.pallas import tpu as pltpu
from jax.sharding import PartitionSpec as P

MESH = pl.DeviceIdType.MESH
PAIR_WIRE = jnp.float32
PART_WIRE = jnp.bfloat16
SUM_WIRE = jnp.bfloat16
FIRST = 0
MOMENT = 2
LATE_OUT = False
VMEM_LIMIT = 32 << 20


def at(start, size):
    return pl.ds(pl.multiple_of(start, 16), size)


def each(count, act):
    def step(index, carry):
        act(index)
        return carry

    lax.fori_loop(1, count, step, 0)


def frames(first, last, act):
    def step(index, carry):
        act(index)
        return carry

    lax.fori_loop(first, last, step, 0)


def columns(rows, width, channels):
    place = lax.broadcasted_iota(jnp.int32, (rows // width, width, channels), 1)
    return place.reshape(rows, channels)


def before(value, place):
    return jnp.where(place == 0, 0.0, pltpu.roll(value, 1, 0))


def after(value, place, width):
    return jnp.where(place == width - 1, 0.0, pltpu.roll(value, value.shape[0] - 1, 0))


def spread(value, place, width):
    kind = jnp.bfloat16
    return jnp.concatenate(
        [after(value, place, width).astype(kind), value.astype(kind), before(value, place).astype(kind)],
        axis=1,
    )


def flat(value):
    return value.reshape(-1, value.shape[-1])


def across(left, right):
    return lax.dot_general(
        left, right, (((1,), (1,)), ((), ())), preferred_element_type=jnp.float32
    )


def contract(left, right):
    return lax.dot_general(
        left, right, (((0,), (0,)), ((), ())), preferred_element_type=jnp.float32
    )


def kernel(
    tiles,
    shards,
    scale,
    latent_ref,
    fwd_ref,
    rev_ref,
    space_hbm,
    time_hbm,
    out_f,
    out_r,
    grad_in,
    grad_s,
    grad_t,
    cells,
    cot_f,
    cot_r,
    acts,
    pre,
    wide,
    rim_out,
    rim_in,
    space_fwd,
    space_back,
    time_back,
    sums,
    pair_out,
    pair_in,
    mid,
    mid_out,
    shard_in,
    total,
    space_ref,
    time_ref,
    load_sem,
    send_sem,
    recv_sem,
):
    tile, shard = lax.axis_index("tile"), lax.axis_index("tm")
    count, height, width, channels = latent_ref.shape
    plane = height * width
    taps = 3

    def tile_peer(step):
        return {"tile": lax.rem(tile + step, tiles)}

    def shard_peer(step):
        return {"tm": lax.rem(shard + step, shards)}

    barrier = pltpu.get_barrier_semaphore()

    def greet(peer):
        pl.semaphore_signal(barrier, inc=1, device_id=peer, device_id_type=MESH)

    each(tiles, lambda step: greet(tile_peer(step)))
    each(shards, lambda step: greet(shard_peer(step)))

    loads = [
        pltpu.make_async_copy(latent_ref, cells.at[:, pl.ds(1, height)], load_sem.at[0]),
        pltpu.make_async_copy(fwd_ref, cot_f.at[pl.ds(0, count)], load_sem.at[1]),
        pltpu.make_async_copy(rev_ref, cot_r.at[pl.ds(2, count)], load_sem.at[2]),
        pltpu.make_async_copy(space_hbm, space_ref, load_sem.at[3]),
        pltpu.make_async_copy(time_hbm, time_ref, load_sem.at[4]),
    ]
    for load in loads:
        load.start()

    has_next_tile, has_last_tile = tile < tiles - 1, tile > 0
    has_next_shard, has_last_shard = shard < shards - 1, shard > 0

    def remote(src, dst, index, peer):
        return pltpu.make_async_remote_copy(
            src_ref=src,
            dst_ref=dst,
            send_sem=send_sem.at[index],
            recv_sem=recv_sem.at[index],
            device_id=peer,
            device_id_type=MESH,
        )

    next_tile, last_tile = tile_peer(1), tile_peer(tiles - 1)
    next_shard, last_shard = shard_peer(1), shard_peer(shards - 1)
    up = (next_tile, has_next_tile, has_last_tile)
    down = (last_tile, has_last_tile, has_next_tile)
    later = (next_shard, has_next_shard, has_last_shard)
    earlier = (last_shard, has_last_shard, has_next_shard)
    moves = [
        (latent_ref.at[:, height - 1], cells.at[:, 0], *up),
        (latent_ref.at[:, 0], cells.at[:, height + 1], *down),
        (fwd_ref.at[0], cot_f.at[count], *earlier),
        (rev_ref.at[count - 1], cot_r.at[1], *later),
        (fwd_ref.at[1], cot_f.at[count + 1], *earlier),
        (rev_ref.at[count - 2], cot_r.at[0], *later),
        (acts.at[count + 1], acts.at[1], *later),
        (acts.at[2], acts.at[count + 2], *earlier),
        (acts.at[count], acts.at[0], *later),
        (acts.at[3], acts.at[count + 3], *earlier),
        (rim_out.at[1], rim_in.at[0], *up),
        (rim_out.at[0], rim_in.at[1], *down),
    ]
    copies = [remote(src, dst, index, peer) for index, (src, dst, peer, _, _) in enumerate(moves)]

    def launch(index):
        pl.when(moves[index][3])(copies[index].start)

    def arrive(index):
        pl.when(moves[index][4])(copies[index].wait_recv)

    def leave(index):
        pl.when(moves[index][3])(copies[index].wait_send)

    for index in range(len(moves)):
        target = moves[index][1]

        @pl.when(jnp.logical_not(moves[index][4]))
        def _(target=target):
            target[...] = jnp.zeros(target.shape, target.dtype)

    sums[...] = jnp.zeros_like(sums)
    loads[3].wait()
    loads[4].wait()
    for row in range(taps):
        time_back[:, row * channels : (row + 1) * channels] = time_ref[
            row * channels : (row + 1) * channels, :
        ]
        time_back[:, (taps + row) * channels : (taps + row + 1) * channels] = time_ref[
            row * channels : (row + 1) * channels, :
        ]
        for col in range(taps):
            index = row * taps + col
            weight = space_ref[index * channels : (index + 1) * channels, :]
            space_fwd[
                row * channels : (row + 1) * channels, col * channels : (col + 1) * channels
            ] = weight
            space_back[:, index * channels : (index + 1) * channels] = weight

    pl.semaphore_wait(barrier, tiles + shards - 2)
    for index in range(6):
        launch(index)
    place = columns(plane, width, channels)

    def window(frame):
        return jnp.concatenate(
            [flat(cells[frame, pl.ds(row, height)]) for row in range(taps)], axis=1
        )

    loads[0].wait()
    arrive(0)
    arrive(1)

    def convolve(frame):
        parts = jnp.dot(window(frame), space_fwd[...], preferred_element_type=jnp.float32)
        value = (
            before(parts[:, :channels], place)
            + parts[:, channels : 2 * channels]
            + after(parts[:, 2 * channels :], place, width)
        )
        pre[frame] = value
        act = value / (1.0 + jnp.exp(-value))
        acts[frame + 2] = act.astype(jnp.bfloat16).reshape(height, width, channels)

    frames(0, count, convolve)

    def second_acts(moment):
        if moment == FIRST:
            launch(6)
            launch(7)
        if moment == MOMENT:
            launch(8)
            launch(9)

    def backward(frame):
        joined = jnp.concatenate(
            [flat(cot_f[frame + lag]) for lag in range(taps)]
            + [flat(cot_r[frame + 2 - lag]) for lag in range(taps)],
            axis=1,
        )
        grad_act = across(joined, time_back[...])
        value = pre[frame]
        gate = 1.0 / (1.0 + jnp.exp(-value))
        grad = grad_act * gate * (1.0 + value * (1.0 - gate))
        grad = grad.astype(jnp.bfloat16).astype(jnp.float32)
        shifted = spread(grad, place, width)
        wide[frame, pl.ds(1, height)] = shifted.reshape(height, width, taps * channels)
        rounded = grad.astype(jnp.bfloat16)
        rim_out[0, frame] = rounded[:width]
        rim_out[1, frame] = rounded[plane - width :]
        lags = contract(flat(acts[frame + 2]), joined)
        for lag in range(taps):
            row = (taps * taps + lag) * channels
            sums[row : row + channels, :] += (
                lags[:, lag * channels : (lag + 1) * channels]
                + lags[:, (taps + lag) * channels : (taps + lag + 1) * channels]
            )
        part = contract(window(frame), shifted)
        for row in range(taps):
            for col in range(taps):
                start = (row * taps + col) * channels
                sums[start : start + channels, :] += part[
                    row * channels : (row + 1) * channels, col * channels : (col + 1) * channels
                ]

    loads[1].wait()
    loads[2].wait()
    arrive(2)
    arrive(3)
    frames(1, count - 1, backward)
    for index in (2, 3, 4, 5):
        leave(index)
    second_acts(0)
    arrive(4)
    arrive(5)
    backward(0)
    backward(count - 1)
    launch(10)
    launch(11)

    half = sums.shape[0] // tiles
    chunk = half // shards

    def settle(phase, ref):
        pltpu.make_async_copy(ref, ref, send_sem.at[phase]).wait()
        pltpu.make_async_copy(ref, ref, recv_sem.at[phase]).wait()

    def rows_to(step):
        return lax.rem(tile + step, tiles) * half

    pair_out[...] = sums[...].astype(PAIR_WIRE)
    each(
        tiles,
        lambda step: remote(
            pair_out.at[at(rows_to(step), half)], pair_in.at[step - 1], 12, tile_peer(step)
        ).start(),
    )

    second_acts(1)

    def outputs(frame):
        base = flat(cells[frame, pl.ds(1, height)]).astype(jnp.float32)
        causal = jnp.concatenate([flat(acts[frame + 2 - lag]) for lag in range(taps)], axis=1)
        anticausal = jnp.concatenate([flat(acts[frame + 2 + lag]) for lag in range(taps)], axis=1)
        for joined, ref in ((causal, out_f), (anticausal, out_r)):
            value = base + jnp.dot(joined, time_ref[...], preferred_element_type=jnp.float32)
            ref[frame] = value.astype(jnp.bfloat16).reshape(height, width, channels)

    def all_outputs():
        for index in range(6, 10):
            arrive(index)
        frames(0, count, outputs)

    def input_grads(frame):
        joined = jnp.concatenate(
            [flat(wide[frame, pl.ds(2 - row, height)]) for row in range(taps)], axis=1
        )
        value = flat(cot_f[frame]).astype(jnp.float32) + flat(cot_r[frame + 2]).astype(jnp.float32)
        value = value + across(joined, space_back[...])
        grad_in[frame] = value.astype(jnp.bfloat16).reshape(height, width, channels)

    settle(12, pair_in)
    own_half = sums[at(tile * half, half), :]
    for index in range(tiles - 1):
        own_half = own_half + pair_in[index].astype(jnp.float32)
    mid[...] = own_half
    mid_out[...] = own_half.astype(PART_WIRE)
    each(
        shards,
        lambda step: remote(
            mid_out.at[at(lax.rem(shard + step, shards) * chunk, chunk)],
            shard_in.at[step - 1],
            13,
            shard_peer(step),
        ).start(),
    )
    second_acts(2)
    settle(13, shard_in)
    part = lax.fori_loop(
        0,
        shards - 1,
        lambda index, value: value + shard_in[index].astype(jnp.float32),
        mid[at(shard * chunk, chunk), :],
    )
    own = at(tile * half + shard * chunk, chunk)
    total[own, :] = (part * scale).astype(SUM_WIRE)
    each(
        shards,
        lambda step: remote(total.at[own], total.at[own], 14, shard_peer(step)).start(),
    )
    second_acts(3)
    arrive(10)
    arrive(11)
    edge = columns(count * width, width, channels)
    for side, row in ((0, 0), (1, height + 1)):
        rim = spread(flat(rim_in[side]).astype(jnp.float32), edge, width)
        wide[:, row] = rim.reshape(count, width, taps * channels)
    frames(0, count, input_grads)
    if not LATE_OUT:
        all_outputs()
    settle(14, total.at[pl.ds(0, (shards - 1) * chunk)])
    mine = at(tile * half, half)
    each(
        tiles,
        lambda step: remote(total.at[mine], total.at[mine], 15, tile_peer(step)).start(),
    )
    if LATE_OUT:
        all_outputs()
    for index in (0, 1, 6, 7, 8, 9, 10, 11):
        leave(index)
    settle(15, total.at[pl.ds(0, (tiles - 1) * half)])
    split = taps * taps * channels
    grad_s[...] = total[:split, :].astype(jnp.float32)
    grad_t[...] = total[split : split + taps * channels, :].astype(jnp.float32)


def deliver_kernel(*refs):
    count = (len(refs) - 1) // 2
    stores = [
        pltpu.make_async_copy(refs[index], refs[count + index], refs[-1].at[index])
        for index in range(count)
    ]
    for store in stores:
        store.start()
    for store in stores:
        store.wait()


def deliver(*values):
    hbm = pl.BlockSpec(memory_space=pl.ANY)
    vmem = pl.BlockSpec(memory_space=pltpu.VMEM)
    count = len(values)
    return pl.pallas_call(
        deliver_kernel,
        out_shape=tuple(jax.ShapeDtypeStruct(value.shape, value.dtype) for value in values),
        in_specs=[vmem] * count,
        out_specs=(hbm,) * count,
        scratch_shapes=[pltpu.SemaphoreType.DMA((count,))],
        compiler_params=pltpu.CompilerParams(vmem_limit_bytes=VMEM_LIMIT),
    )(*(pltpu.with_memory_space_constraint(value, pltpu.VMEM) for value in values))


def body(latent, cot_forward, cot_reverse, spatial_weight, temporal_weight):
    tiles, shards = lax.axis_size("tile"), lax.axis_size("tm")
    count, height, width, channels = latent.shape
    positions = count * height * width * shards * tiles
    scale = 1.0 / math.sqrt(positions)
    rows = 12 * channels
    unit = 16 * tiles * shards
    padded = -(-rows // unit) * unit
    half = padded // tiles
    chunk = half // shards
    kind = jnp.bfloat16
    vmem = pl.BlockSpec(memory_space=pltpu.VMEM)
    hbm = pl.BlockSpec(memory_space=pltpu.HBM)
    results = pl.pallas_call(
        functools.partial(kernel, tiles, shards, scale),
        out_shape=(
            pltpu.VMEM(latent.shape, kind),
            pltpu.VMEM(latent.shape, kind),
            pltpu.VMEM(latent.shape, kind),
            pltpu.VMEM((9 * channels, channels), jnp.float32),
            pltpu.VMEM((3 * channels, channels), jnp.float32),
        ),
        in_specs=[hbm] * 5,
        out_specs=(vmem,) * 5,
        scratch_shapes=[
            pltpu.VMEM((count, height + 2, width, channels), kind),
            pltpu.VMEM((count + 2, height, width, channels), kind),
            pltpu.VMEM((count + 2, height, width, channels), kind),
            pltpu.VMEM((count + 4, height, width, channels), kind),
            pltpu.VMEM((count, height * width, channels), jnp.float32),
            pltpu.VMEM((count, height + 2, width, 3 * channels), kind),
            pltpu.VMEM((2, count, width, channels), kind),
            pltpu.VMEM((2, count, width, channels), kind),
            pltpu.VMEM((3 * channels, 3 * channels), kind),
            pltpu.VMEM((channels, 9 * channels), kind),
            pltpu.VMEM((channels, 6 * channels), kind),
            pltpu.VMEM((padded, channels), jnp.float32),
            pltpu.VMEM((padded, channels), PAIR_WIRE),
            pltpu.VMEM((tiles - 1, half, channels), PAIR_WIRE),
            pltpu.VMEM((half, channels), jnp.float32),
            pltpu.VMEM((half, channels), PART_WIRE),
            pltpu.VMEM((shards - 1, chunk, channels), PART_WIRE),
            pltpu.VMEM((padded, channels), SUM_WIRE),
            pltpu.VMEM((9 * channels, channels), kind),
            pltpu.VMEM((3 * channels, channels), kind),
            pltpu.SemaphoreType.DMA((5,)),
            pltpu.SemaphoreType.DMA((16,)),
            pltpu.SemaphoreType.DMA((16,)),
        ],
        compiler_params=pltpu.CompilerParams(collective_id=0, has_side_effects=True, vmem_limit_bytes=VMEM_LIMIT),
    )(
        *(
            pltpu.with_memory_space_constraint(value, pltpu.HBM)
            for value in (
                latent,
                cot_forward,
                cot_reverse,
                spatial_weight.reshape(9 * channels, channels),
                temporal_weight.reshape(3 * channels, channels),
            )
        ),
    )
    out_f, out_r, grad_in, grad_s, grad_t = deliver(*results)
    return (
        out_f,
        out_r,
        grad_in,
        grad_s.reshape(spatial_weight.shape),
        grad_t.reshape(temporal_weight.shape),
    )


def solution(mesh):
    placed = (
        P("tm", "tile", None, None),
        P("tm", "tile", None, None),
        P("tm", "tile", None, None),
        P(),
        P(),
    )
    return jax.shard_map(
        body,
        mesh=mesh,
        in_specs=placed,
        out_specs=(
            P("tm", "tile", None, None),
            P("tm", "tile", None, None),
            P("tm", "tile", None, None),
            P(),
            P(),
        ),
        check_vma=False,
    )
```

```python
import functools
import math

import jax
import jax.numpy as jnp
from jax import lax
from jax.experimental import pallas as pl
from jax.experimental.pallas import tpu as pltpu
from jax.sharding import PartitionSpec as P

MESH = pl.DeviceIdType.MESH
KIND = jnp.bfloat16
TAPS = 3
REACH = TAPS - 1
PIECES = 2
PARTS = 2
ACTS_AT = (4, 6, 8)
VMEM_LIMIT = 32 << 20


def at(start, size):
    return pl.ds(pl.multiple_of(start, 16), size)


def each(count, act):
    def step(index, carry):
        act(index)
        return carry

    lax.fori_loop(1, count, step, 0)


def frames(first, last, act):
    def step(index, carry):
        act(index)
        return carry

    lax.fori_loop(first, last, step, 0)


def columns(rows, width, channels):
    place = lax.broadcasted_iota(jnp.int32, (rows // width, width, channels), 1)
    return place.reshape(rows, channels)


def before(value, place):
    return jnp.where(place == 0, 0.0, pltpu.roll(value, 1, 0))


def after(value, place, width):
    return jnp.where(place == width - 1, 0.0, pltpu.roll(value, value.shape[0] - 1, 0))


def spread(value, place, width):
    return jnp.concatenate(
        [after(value, place, width).astype(KIND), value.astype(KIND), before(value, place).astype(KIND)],
        axis=1,
    )


def flat(value):
    return value.reshape(-1, value.shape[-1])


def across(left, right):
    return lax.dot_general(
        left, right, (((1,), (1,)), ((), ())), preferred_element_type=jnp.float32
    )


def contract(left, right):
    return lax.dot_general(
        left, right, (((0,), (0,)), ((), ())), preferred_element_type=jnp.float32
    )


def kernel(
    tiles,
    shards,
    scale,
    latent_ref,
    fwd_ref,
    rev_ref,
    space_hbm,
    time_hbm,
    out_f,
    out_r,
    grad_in,
    grad_s,
    grad_t,
    cells,
    cot_f,
    cot_r,
    acts,
    gates,
    pulls,
    wide,
    rim_out,
    rim_in,
    space_ref,
    time_ref,
    space_fwd,
    space_back,
    time_back,
    sums,
    pair_in,
    mid,
    mid_out,
    shard_in,
    mate_out,
    mate_in,
    total,
    load_sem,
    ready,
    halo_send,
    halo_recv,
    sum_send,
    sum_recv,
):
    tile, shard = lax.axis_index("tile"), lax.axis_index("tm")
    count, height, width, channels = latent_ref.shape
    plane = height * width
    mates = 2 if shards % 2 == 0 else 1
    crew = shards // mates

    def tile_peer(step):
        return {"tile": lax.rem(tile + step, tiles)}

    def shard_peer(step):
        return {"tm": lax.rem(shard + step, shards)}

    def crew_peer(step):
        return {"tm": lax.rem(shard + step * mates, shards)}

    def signal(semaphore, peer):
        pl.semaphore_signal(semaphore, inc=1, device_id=peer, device_id_type=MESH)

    loads = [
        pltpu.make_async_copy(src, dst, load_sem.at[index])
        for index, (src, dst) in enumerate(
            (
                (space_hbm, space_ref),
                (time_hbm, time_ref),
                (latent_ref, cells.at[:, pl.ds(1, height)]),
                (fwd_ref, cot_f.at[pl.ds(0, count)]),
                (rev_ref, cot_r.at[pl.ds(REACH, count)]),
            )
        )
    ]
    barrier = pltpu.get_barrier_semaphore()
    signal(barrier, shard_peer(1))
    signal(barrier, shard_peer(shards - 1))
    each(tiles, lambda step: signal(barrier, tile_peer(step)))
    for load in loads:
        load.start()

    has_next_tile, has_last_tile = tile < tiles - 1, tile > 0
    has_next_shard, has_last_shard = shard < shards - 1, shard > 0

    next_tile, last_tile = tile_peer(1), tile_peer(tiles - 1)
    next_shard, last_shard = shard_peer(1), shard_peer(shards - 1)
    up = (next_tile, has_next_tile, has_last_tile)
    down = (last_tile, has_last_tile, has_next_tile)
    later = (next_shard, has_next_shard, has_last_shard)
    earlier = (last_shard, has_last_shard, has_next_shard)
    moves = []

    def move(src, dst, way):
        moves.append((src, dst, *way))
        return len(moves) - 1

    cell_moves = [
        move(latent_ref.at[:, height - 1], cells.at[:, 0], up),
        move(latent_ref.at[:, 0], cells.at[:, height + 1], down),
    ]
    cot_moves = []
    for reach in range(REACH):
        cot_moves.append(
            [
                move(fwd_ref.at[reach], cot_f.at[count + reach], earlier),
                move(rev_ref.at[count - 1 - reach], cot_r.at[REACH - 1 - reach], later),
            ]
        )
    rim_moves = [move(rim_out.at[1], rim_in.at[0], up), move(rim_out.at[0], rim_in.at[1], down)]
    parts = PARTS if height % PARTS == 0 else 1
    rows = height // parts
    act_moves = []
    for reach in range(REACH):
        group = []
        for part in range(parts):
            cut = pl.ds(part * rows, rows)
            group.append(
                move(acts.at[count + 1 - reach, cut], acts.at[1 - reach, cut], later)
            )
            group.append(
                move(acts.at[REACH + reach, cut], acts.at[count + REACH + reach, cut], earlier)
            )
        act_moves.append(group)
    act_order = [index for group in act_moves for index in group]

    def remote(src, dst, send, recv, peer):
        return pltpu.make_async_remote_copy(
            src_ref=src, dst_ref=dst, send_sem=send, recv_sem=recv, device_id=peer, device_id_type=MESH
        )

    copies = [
        remote(src, dst, halo_send.at[index], halo_recv.at[index], peer)
        for index, (src, dst, peer, _, _) in enumerate(moves)
    ]

    def launch(indices):
        for index in indices:
            pl.when(moves[index][3])(copies[index].start)

    def arrive(indices):
        for index in indices:
            pl.when(moves[index][4])(copies[index].wait_recv)

    def leave(indices):
        for index in indices:
            pl.when(moves[index][3])(copies[index].wait_send)

    pl.semaphore_wait(barrier, tiles + 1)
    for group in cot_moves:
        launch(group)
    launch(cell_moves)
    spans = []
    span = 1
    while span * 2 < shards:
        spans.append(span)
        span *= 2

    def tell(index):
        signal(ready.at[index], shard_peer(spans[index]))
        signal(ready.at[index], shard_peer(shards - spans[index]))

    def hear(index):
        pl.semaphore_wait(ready.at[index], 2)

    tell(0)
    for index in range(len(moves)):
        target = moves[index][1]

        @pl.when(jnp.logical_not(moves[index][4]))
        def _(target=target):
            target[...] = jnp.zeros(target.shape, target.dtype)

    sums[...] = jnp.zeros_like(sums)
    place = columns(plane, width, channels)
    loads[0].wait()
    loads[1].wait()

    def block(index):
        return slice(index * channels, (index + 1) * channels)

    for row in range(TAPS):
        weight = time_ref[block(row), :]
        time_back[:, block(REACH - row)] = weight
        time_back[:, block(TAPS + row)] = weight
        for col in range(TAPS):
            weight = space_ref[block(row * TAPS + col), :]
            space_fwd[block(row), block(col)] = weight
            space_back[:, block(row * TAPS + col)] = weight

    def window(frame):
        return jnp.concatenate(
            [flat(cells[frame, pl.ds(row, height)]) for row in range(TAPS)], axis=1
        )

    loads[2].wait()
    arrive(cell_moves)

    def convolve(frame):
        taken = jnp.dot(window(frame), space_fwd[...], preferred_element_type=jnp.float32)
        value = (
            before(taken[:, :channels], place)
            + taken[:, channels : 2 * channels]
            + after(taken[:, 2 * channels :], place, width)
        )
        share = 1.0 / (1.0 + jnp.exp(-value))
        gates[frame] = share * (1.0 + value * (1.0 - share))
        act = value * share
        acts[frame + REACH] = act.astype(KIND).reshape(height, width, channels)

    frames(0, count, convolve)
    hear(0)
    for index in range(1, len(spans)):
        if index == 1:
            tell(1)
    sent = [0]

    def send_acts(moment):
        upto = min(ACTS_AT[moment] * len(act_order) // 8, len(act_order))
        launch(act_order[sent[0] : upto])
        sent[0] = upto

    send_acts(0)

    def add_lag(lag, value):
        sums[0, block(lag), :] += value

    def own_pull(frame):
        low = max(0, frame + REACH - (count - 1))
        high = min(REACH, frame)
        fwd = [flat(cot_f[frame + lag]) for lag in range(REACH - low, -1, -1)]
        rev = [flat(cot_r[frame + REACH - lag]) for lag in range(high + 1)]
        joined = jnp.concatenate(fwd + rev, axis=1)
        columns_of = slice(low * channels, (TAPS + high + 1) * channels)
        pulls[frame] = across(joined, time_back[:, columns_of])
        lags = contract(flat(acts[frame + REACH]), joined)
        for index in range(len(fwd)):
            add_lag(REACH - low - index, lags[:, block(index)])
        for lag in range(high + 1):
            add_lag(lag, lags[:, block(len(fwd) + lag)])

    loads[3].wait()
    loads[4].wait()
    for frame in range(count):
        own_pull(frame)
    for index in range(1, len(spans)):
        hear(index)
        if index + 1 < len(spans):
            tell(index + 1)

    def stage_of(frame):
        return max(0, REACH - frame, REACH - (count - 1 - frame))

    def halo_terms(frame, reach):
        terms = []
        lag = frame + reach
        if lag <= REACH:
            terms.append((lag, cot_r, REACH - reach))
        lag = count - 1 - frame + reach
        if lag <= REACH:
            terms.append((lag, cot_f, count + reach - 1))
        return terms

    def pull_halo(frame, reach):
        for lag, source, index in halo_terms(frame, reach):
            taken = flat(source[index])
            pulls[frame] += across(taken, time_back[:, block(TAPS + lag)])
            add_lag(lag, contract(flat(acts[frame + REACH]), taken))

    def settle_frame(frame):
        grad = (pulls[frame] * gates[frame]).astype(KIND)
        shifted = spread(grad.astype(jnp.float32), place, width)
        wide[frame, pl.ds(1, height)] = shifted.reshape(height, width, TAPS * channels)
        rim_out[0, frame] = grad[:width]
        rim_out[1, frame] = grad[plane - width :]
        part = contract(window(frame), shifted)
        for row in range(TAPS):
            for col in range(TAPS):
                tap = TAPS + row * TAPS + col
                spot = block(tap % (4 * TAPS // PIECES))
                sums[tap // (4 * TAPS // PIECES), spot, :] += part[block(row), block(col)]

    for frame in range(count):
        if stage_of(frame) == 0:
            settle_frame(frame)
    for reach in range(1, REACH + 1):
        arrive(cot_moves[reach - 1])
        for frame in range(count):
            if stage_of(frame) >= reach:
                pull_halo(frame, reach)
                if stage_of(frame) == reach:
                    settle_frame(frame)

    half = sums.shape[1] // tiles
    chunk = half // crew
    rank = shard // mates

    def settle(phase, piece, ref):
        spot = phase * PIECES + piece
        pltpu.make_async_copy(ref, ref, sum_send.at[spot]).wait()
        pltpu.make_async_copy(ref, ref, sum_recv.at[spot]).wait()

    def pass_on(phase, piece, src, dst, peer):
        spot = phase * PIECES + piece
        remote(src, dst, sum_send.at[spot], sum_recv.at[spot], peer).start()

    mine = at(tile * half, half)
    own = at(tile * half + rank * chunk, chunk)

    for piece in range(PIECES):
        each(
            tiles,
            lambda step, piece=piece: pass_on(
                0,
                piece,
                sums.at[piece, at(lax.rem(tile + step, tiles) * half, half)],
                pair_in.at[piece, step - 1],
                tile_peer(step),
            ),
        )
    launch(rim_moves)

    def out_forward(frame):
        joined = jnp.concatenate([flat(acts[frame + REACH - lag]) for lag in range(TAPS)], axis=1)
        value = flat(cells[frame, pl.ds(1, height)]).astype(jnp.float32)
        value = value + jnp.dot(joined, time_ref[...], preferred_element_type=jnp.float32)
        out_f[frame] = value.astype(KIND).reshape(height, width, channels)

    def out_reverse(frame):
        joined = jnp.concatenate([flat(acts[frame + REACH + lag]) for lag in range(TAPS)], axis=1)
        value = flat(cells[frame, pl.ds(1, height)]).astype(jnp.float32)
        value = value + jnp.dot(joined, time_ref[...], preferred_element_type=jnp.float32)
        out_r[frame] = value.astype(KIND).reshape(height, width, channels)

    def outputs(reach):
        for frame in range(count):
            if max(0, REACH - frame) == reach:
                out_forward(frame)
            if max(0, REACH - (count - 1 - frame)) == reach:
                out_reverse(frame)

    outputs(0)

    def scatter(piece):
        settle(0, piece, pair_in.at[piece])
        value = sums[piece, mine, :]
        for index in range(tiles - 1):
            value = value + pair_in[piece, index]
        mid[piece] = value
        mid_out[piece] = value.astype(KIND)
        each(
            crew,
            lambda step: pass_on(
                1,
                piece,
                mid_out.at[piece, at(lax.rem(rank + step, crew) * chunk, chunk)],
                shard_in.at[piece, step - 1],
                crew_peer(step),
            ),
        )

    for piece in range(PIECES):
        scatter(piece)
    send_acts(1)

    arrive(rim_moves)
    edge = columns(count * width, width, channels)
    for side, row in ((0, 0), (1, height + 1)):
        rim = spread(flat(rim_in[side]).astype(jnp.float32), edge, width)
        wide[:, row] = rim.reshape(count, width, TAPS * channels)

    def input_grads(frame):
        joined = jnp.concatenate(
            [flat(wide[frame, pl.ds(2 - row, height)]) for row in range(TAPS)], axis=1
        )
        value = flat(cot_f[frame]).astype(jnp.float32) + flat(cot_r[frame + REACH]).astype(jnp.float32)
        value = value + across(joined, space_back[...])
        grad_in[frame] = value.astype(KIND).reshape(height, width, channels)

    frames(0, count, input_grads)

    def share_mates(piece):
        settle(1, piece, shard_in.at[piece])
        value = lax.fori_loop(
            0,
            crew - 1,
            lambda index, value: value + shard_in[piece, index].astype(jnp.float32),
            mid[piece, at(rank * chunk, chunk), :],
        )
        mate_out[piece] = value
        if mates == 2:
            pass_on(
                2,
                piece,
                mate_out.at[piece],
                mate_in.at[piece],
                {"tm": shard + 1 - 2 * lax.rem(shard, 2)},
            )

    for piece in range(PIECES):
        share_mates(piece)
    send_acts(2)

    def gather(piece):
        value = mate_out[piece]
        if mates == 2:
            settle(2, piece, mate_in.at[piece])
            value = value + mate_in[piece]
        total[piece, own, :] = (value * scale).astype(KIND)
        each(
            crew,
            lambda step: pass_on(
                3, piece, total.at[piece, own], total.at[piece, own], crew_peer(step)
            ),
        )

    for piece in range(PIECES):
        gather(piece)

    arrive(act_moves[0])
    outputs(1)

    def forward_piece(piece):
        settle(3, piece, total.at[piece, pl.ds(0, (crew - 1) * chunk)])
        each(
            tiles,
            lambda step: pass_on(
                4, piece, total.at[piece, mine], total.at[piece, mine], tile_peer(step)
            ),
        )

    for piece in range(PIECES):
        forward_piece(piece)
    for reach in range(1, REACH):
        arrive(act_moves[reach])
        outputs(reach + 1)
    for piece in range(PIECES):
        settle(4, piece, total.at[piece, pl.ds(0, (tiles - 1) * half)])
    for tap in range(4 * TAPS):
        value = total[tap // (4 * TAPS // PIECES), block(tap % (4 * TAPS // PIECES)), :].astype(jnp.float32)
        if tap < TAPS:
            grad_t[block(tap), :] = value
        else:
            grad_s[block(tap - TAPS), :] = value
    leave(range(len(moves)))


def deliver_kernel(*refs):
    count = (len(refs) - 1) // 2
    stores = [
        pltpu.make_async_copy(refs[index], refs[count + index], refs[-1].at[index])
        for index in range(count)
    ]
    for store in stores:
        store.start()
    for store in stores:
        store.wait()


def deliver(*values):
    hbm = pl.BlockSpec(memory_space=pl.ANY)
    vmem = pl.BlockSpec(memory_space=pltpu.VMEM)
    count = len(values)
    return pl.pallas_call(
        deliver_kernel,
        out_shape=tuple(jax.ShapeDtypeStruct(value.shape, value.dtype) for value in values),
        in_specs=[vmem] * count,
        out_specs=(hbm,) * count,
        scratch_shapes=[pltpu.SemaphoreType.DMA((count,))],
        compiler_params=pltpu.CompilerParams(vmem_limit_bytes=VMEM_LIMIT),
    )(*(pltpu.with_memory_space_constraint(value, pltpu.VMEM) for value in values))


def body(latent, cot_forward, cot_reverse, spatial_weight, temporal_weight):
    tiles, shards = lax.axis_size("tile"), lax.axis_size("tm")
    count, height, width, channels = latent.shape
    positions = count * height * width * shards * tiles
    scale = 1.0 / math.sqrt(positions)
    mates = 2 if shards % 2 == 0 else 1
    crew = shards // mates
    rows = 4 * TAPS * channels // PIECES
    unit = 16 * tiles * crew
    padded = -(-rows // unit) * unit
    half = padded // tiles
    chunk = half // crew
    stages = max(1, (shards - 1).bit_length() - 1)
    parts = PARTS if height % PARTS == 0 else 1
    moves = 4 + REACH * 2 + REACH * 2 * parts
    vmem = pl.BlockSpec(memory_space=pltpu.VMEM)
    hbm = pl.BlockSpec(memory_space=pltpu.HBM)
    results = pl.pallas_call(
        functools.partial(kernel, tiles, shards, scale),
        out_shape=(
            pltpu.VMEM(latent.shape, KIND),
            pltpu.VMEM(latent.shape, KIND),
            pltpu.VMEM(latent.shape, KIND),
            pltpu.VMEM((9 * channels, channels), jnp.float32),
            pltpu.VMEM((3 * channels, channels), jnp.float32),
        ),
        in_specs=[hbm] * 5,
        out_specs=(vmem,) * 5,
        scratch_shapes=[
            pltpu.VMEM((count, height + 2, width, channels), KIND),
            pltpu.VMEM((count + REACH, height, width, channels), KIND),
            pltpu.VMEM((count + REACH, height, width, channels), KIND),
            pltpu.VMEM((count + 2 * REACH, height, width, channels), KIND),
            pltpu.VMEM((count, height * width, channels), jnp.float32),
            pltpu.VMEM((count, height * width, channels), jnp.float32),
            pltpu.VMEM((count, height + 2, width, TAPS * channels), KIND),
            pltpu.VMEM((2, count, width, channels), KIND),
            pltpu.VMEM((2, count, width, channels), KIND),
            pltpu.VMEM((9 * channels, channels), KIND),
            pltpu.VMEM((3 * channels, channels), KIND),
            pltpu.VMEM((3 * channels, 3 * channels), KIND),
            pltpu.VMEM((channels, 9 * channels), KIND),
            pltpu.VMEM((channels, 6 * channels), KIND),
            pltpu.VMEM((PIECES, padded, channels), jnp.float32),
            pltpu.VMEM((PIECES, tiles - 1, half, channels), jnp.float32),
            pltpu.VMEM((PIECES, half, channels), jnp.float32),
            pltpu.VMEM((PIECES, half, channels), KIND),
            pltpu.VMEM((PIECES, crew - 1, chunk, channels), KIND),
            pltpu.VMEM((PIECES, chunk, channels), jnp.float32),
            pltpu.VMEM((PIECES, chunk, channels), jnp.float32),
            pltpu.VMEM((PIECES, padded, channels), KIND),
            pltpu.SemaphoreType.DMA((5,)),
            pltpu.SemaphoreType.REGULAR((stages,)),
            pltpu.SemaphoreType.DMA((moves,)),
            pltpu.SemaphoreType.DMA((moves,)),
            pltpu.SemaphoreType.DMA((5 * PIECES,)),
            pltpu.SemaphoreType.DMA((5 * PIECES,)),
        ],
        compiler_params=pltpu.CompilerParams(
            collective_id=0, has_side_effects=True, vmem_limit_bytes=VMEM_LIMIT
        ),
    )(
        *(
            pltpu.with_memory_space_constraint(value, pltpu.HBM)
            for value in (
                latent,
                cot_forward,
                cot_reverse,
                spatial_weight.reshape(9 * channels, channels),
                temporal_weight.reshape(3 * channels, channels),
            )
        ),
    )
    out_f, out_r, grad_in, grad_s, grad_t = deliver(*results)
    return (
        out_f,
        out_r,
        grad_in,
        grad_s.reshape(spatial_weight.shape),
        grad_t.reshape(temporal_weight.shape),
    )


def solution(mesh):
    split, copied = P("tm", "tile", None, None), P()
    return jax.shard_map(
        body,
        mesh=mesh,
        in_specs=(split, split, split, copied, copied),
        out_specs=(split, split, split, copied, copied),
        check_vma=False,
    )
```

```python
import functools
import math

import jax
import jax.numpy as jnp
from jax import lax
from jax.experimental import pallas as pl
from jax.experimental.pallas import tpu as pltpu
from jax.sharding import PartitionSpec as P

MESH = pl.DeviceIdType.MESH
KIND = jnp.bfloat16
TAPS = 3
REACH = TAPS - 1
PIECES = 1
PARTS = 2
MATES = 1
HOLD = 1
ACTS_AT = (0,0,4,4,8,8,12,16)
ACTS_IN = (0,4,4,4,10,10,12,16)
VMEM_LIMIT = 32 << 20


def at(start, size):
    return pl.ds(pl.multiple_of(start, 16), size)


def each(count, act):
    def step(index, carry):
        act(index)
        return carry

    lax.fori_loop(1, count, step, 0)


def frames(first, last, act):
    def step(index, carry):
        act(index)
        return carry

    lax.fori_loop(first, last, step, 0)


def columns(rows, width, channels):
    place = lax.broadcasted_iota(jnp.int32, (rows // width, width, channels), 1)
    return place.reshape(rows, channels)


def before(value, place):
    return jnp.where(place == 0, 0.0, pltpu.roll(value, 1, 0))


def after(value, place, width):
    return jnp.where(place == width - 1, 0.0, pltpu.roll(value, value.shape[0] - 1, 0))


def spread(value, place, width):
    return jnp.concatenate(
        [after(value, place, width).astype(KIND), value.astype(KIND), before(value, place).astype(KIND)],
        axis=1,
    )


def flat(value):
    return value.reshape(-1, value.shape[-1])


def across(left, right):
    return lax.dot_general(
        left, right, (((1,), (1,)), ((), ())), preferred_element_type=jnp.float32
    )


def contract(left, right):
    return lax.dot_general(
        left, right, (((0,), (0,)), ((), ())), preferred_element_type=jnp.float32
    )


def kernel(
    tiles,
    shards,
    scale,
    latent_ref,
    fwd_ref,
    rev_ref,
    space_hbm,
    time_hbm,
    out_f,
    out_r,
    grad_in,
    grad_s,
    grad_t,
    cells,
    cot_f,
    cot_r,
    acts,
    gates,
    pulls,
    wide,
    rim_out,
    rim_in,
    space_ref,
    time_ref,
    space_fwd,
    space_back,
    time_back,
    sums,
    pair_in,
    mid,
    mid_out,
    shard_in,
    mate_out,
    mate_in,
    total,
    load_sem,
    ready,
    halo_send,
    halo_recv,
    sum_send,
    sum_recv,
):
    tile, shard = lax.axis_index("tile"), lax.axis_index("tm")
    count, height, width, channels = latent_ref.shape
    plane = height * width
    mates = MATES if shards % MATES == 0 else 1
    crew = shards // mates

    def tile_peer(step):
        return {"tile": lax.rem(tile + step, tiles)}

    def shard_peer(step):
        return {"tm": lax.rem(shard + step, shards)}

    def crew_peer(step):
        return {"tm": lax.rem(shard + step * mates, shards)}

    def signal(semaphore, peer):
        pl.semaphore_signal(semaphore, inc=1, device_id=peer, device_id_type=MESH)

    loads = [
        pltpu.make_async_copy(src, dst, load_sem.at[index])
        for index, (src, dst) in enumerate(
            (
                (space_hbm, space_ref),
                (time_hbm, time_ref),
                (latent_ref, cells.at[:, pl.ds(1, height)]),
                (fwd_ref, cot_f.at[pl.ds(0, count)]),
                (rev_ref, cot_r.at[pl.ds(REACH, count)]),
            )
        )
    ]
    barrier = pltpu.get_barrier_semaphore()
    has_next_tile, has_last_tile = tile < tiles - 1, tile > 0
    has_next_shard, has_last_shard = shard < shards - 1, shard > 0

    def around(semaphore, span):
        pl.when(shard + span < shards)(lambda: signal(semaphore, {"tm": shard + span}))
        pl.when(shard >= span)(lambda: signal(semaphore, {"tm": shard - span}))

    def near(span):
        return (shard + span < shards).astype(jnp.int32) + (shard >= span).astype(jnp.int32)

    around(barrier, 1)
    each(tiles, lambda step: signal(barrier, tile_peer(step)))
    for load in loads:
        load.start()

    next_tile, last_tile = tile_peer(1), tile_peer(tiles - 1)
    next_shard, last_shard = shard_peer(1), shard_peer(shards - 1)
    up = (next_tile, has_next_tile, has_last_tile)
    down = (last_tile, has_last_tile, has_next_tile)
    later = (next_shard, has_next_shard, has_last_shard)
    earlier = (last_shard, has_last_shard, has_next_shard)
    moves = []

    def move(src, dst, way):
        moves.append((src, dst, *way))
        return len(moves) - 1

    cell_moves = [
        move(latent_ref.at[:, height - 1], cells.at[:, 0], up),
        move(latent_ref.at[:, 0], cells.at[:, height + 1], down),
    ]
    cot_moves = []
    for reach in range(REACH):
        cot_moves.append(
            [
                move(fwd_ref.at[reach], cot_f.at[count + reach], earlier),
                move(rev_ref.at[count - 1 - reach], cot_r.at[REACH - 1 - reach], later),
            ]
        )
    rim_moves = [move(rim_out.at[1], rim_in.at[0], up), move(rim_out.at[0], rim_in.at[1], down)]
    parts = PARTS if height % PARTS == 0 else 1
    rows = height // parts
    act_moves = []
    for reach in range(REACH):
        group = []
        for part in range(parts):
            cut = pl.ds(part * rows, rows)
            group.append(
                move(acts.at[count + 1 - reach, cut], acts.at[1 - reach, cut], later)
            )
            group.append(
                move(acts.at[REACH + reach, cut], acts.at[count + REACH + reach, cut], earlier)
            )
        act_moves.append(group)
    act_order = [index for group in act_moves for index in group]

    def remote(src, dst, send, recv, peer):
        return pltpu.make_async_remote_copy(
            src_ref=src, dst_ref=dst, send_sem=send, recv_sem=recv, device_id=peer, device_id_type=MESH
        )

    copies = [
        remote(src, dst, halo_send.at[index], halo_recv.at[index], peer)
        for index, (src, dst, peer, _, _) in enumerate(moves)
    ]

    def launch(indices, only=None):
        for index in indices:
            ready_to = moves[index][3]
            if only is not None:
                ready_to = jnp.logical_and(ready_to, only)
            pl.when(ready_to)(copies[index].start)

    def arrive(indices):
        for index in indices:
            pl.when(moves[index][4])(copies[index].wait_recv)

    def leave(indices):
        for index in indices:
            pl.when(moves[index][3])(copies[index].wait_send)

    pl.semaphore_wait(barrier, tiles - 1 + near(1))
    corner = (lax.rem(shard, 4) == 0, lax.rem(shard, 4) == 3)
    launch(cell_moves)
    launch(cot_moves[0])
    for group in cot_moves[1:]:
        for index, held in zip(group, corner):
            launch([index], jnp.logical_not(held) if HOLD else None)
    spans = []
    span = 1
    while span < shards - 1:
        spans.append(span)
        span *= 2

    def tell(index):
        around(ready.at[index], spans[index])

    def hear(index):
        pl.semaphore_wait(ready.at[index], near(spans[index]))

    tell(0)
    for index in range(len(moves)):
        target = moves[index][1]

        @pl.when(jnp.logical_not(moves[index][4]))
        def _(target=target):
            target[...] = jnp.zeros(target.shape, target.dtype)

    sums[...] = jnp.zeros_like(sums)
    place = columns(plane, width, channels)
    loads[0].wait()
    loads[1].wait()

    def block(index):
        return slice(index * channels, (index + 1) * channels)

    for row in range(TAPS):
        weight = time_ref[block(row), :]
        time_back[:, block(REACH - row)] = weight
        time_back[:, block(TAPS + row)] = weight
        for col in range(TAPS):
            weight = space_ref[block(row * TAPS + col), :]
            space_fwd[block(row), block(col)] = weight
            space_back[:, block(row * TAPS + col)] = weight

    def window(frame):
        return jnp.concatenate(
            [flat(cells[frame, pl.ds(row, height)]) for row in range(TAPS)], axis=1
        )

    loads[2].wait()
    arrive(cell_moves)

    def convolve(frame):
        taken = jnp.dot(window(frame), space_fwd[...], preferred_element_type=jnp.float32)
        value = (
            before(taken[:, :channels], place)
            + taken[:, channels : 2 * channels]
            + after(taken[:, 2 * channels :], place, width)
        )
        share = 1.0 / (1.0 + jnp.exp(-value))
        gates[frame] = share * (1.0 + value * (1.0 - share))
        act = value * share
        acts[frame + REACH] = act.astype(KIND).reshape(height, width, channels)

    frames(0, count, convolve)
    hear(0)
    for index in range(1, len(spans)):
        if index == 1:
            tell(1)
    inner = lax.rem(shard + shard // 2, 2) == 1

    def send_acts(moment):
        for kind, table in ((inner, ACTS_IN), (jnp.logical_not(inner), ACTS_AT)):
            first, last = (
                table[index] * len(act_order) // 16 if index >= 0 else 0
                for index in (moment - 1, moment)
            )
            if last > first:
                pl.when(kind)(functools.partial(launch, act_order[first:last]))

    send_acts(0)

    def add_lag(lag, value):
        sums[0, block(lag), :] += value

    def own_pull(frame):
        low = max(0, frame + REACH - (count - 1))
        high = min(REACH, frame)
        fwd = [flat(cot_f[frame + lag]) for lag in range(REACH - low, -1, -1)]
        rev = [flat(cot_r[frame + REACH - lag]) for lag in range(high + 1)]
        joined = jnp.concatenate(fwd + rev, axis=1)
        columns_of = slice(low * channels, (TAPS + high + 1) * channels)
        pulls[frame] = across(joined, time_back[:, columns_of])
        lags = contract(flat(acts[frame + REACH]), joined)
        for index in range(len(fwd)):
            add_lag(REACH - low - index, lags[:, block(index)])
        for lag in range(high + 1):
            add_lag(lag, lags[:, block(len(fwd) + lag)])

    loads[3].wait()
    loads[4].wait()
    for frame in range(count):
        own_pull(frame)
    for index in range(1, len(spans)):
        hear(index)
        if index + 1 < len(spans):
            tell(index + 1)

    def stage_of(frame):
        return max(0, REACH - frame, REACH - (count - 1 - frame))

    def halo_terms(frame, reach):
        terms = []
        lag = frame + reach
        if lag <= REACH:
            terms.append((lag, cot_r, REACH - reach))
        lag = count - 1 - frame + reach
        if lag <= REACH:
            terms.append((lag, cot_f, count + reach - 1))
        return terms

    def pull_halo(frame, reach):
        for lag, source, index in halo_terms(frame, reach):
            taken = flat(source[index])
            pulls[frame] += across(taken, time_back[:, block(TAPS + lag)])
            add_lag(lag, contract(flat(acts[frame + REACH]), taken))

    def settle_frame(frame):
        grad = (pulls[frame] * gates[frame]).astype(KIND)
        shifted = spread(grad.astype(jnp.float32), place, width)
        wide[frame, pl.ds(1, height)] = shifted.reshape(height, width, TAPS * channels)
        rim_out[0, frame] = grad[:width]
        rim_out[1, frame] = grad[plane - width :]
        part = contract(window(frame), shifted)
        for row in range(TAPS):
            for col in range(TAPS):
                tap = TAPS + row * TAPS + col
                spot = block(tap % (4 * TAPS // PIECES))
                sums[tap // (4 * TAPS // PIECES), spot, :] += part[block(row), block(col)]

    for frame in range(count):
        if stage_of(frame) == 0:
            settle_frame(frame)
    for reach in range(1, REACH + 1):
        arrive(cot_moves[reach - 1])
        if reach == 1 and HOLD == 1:
            for group in cot_moves[1:]:
                for index, held in zip(group, corner):
                    launch([index], held)
        if reach == REACH:
            send_acts(1)
        for frame in range(count):
            if stage_of(frame) >= reach:
                pull_halo(frame, reach)
                if stage_of(frame) == reach:
                    settle_frame(frame)
        if reach == 1 and HOLD == 2:
            for group in cot_moves[1:]:
                for index, held in zip(group, corner):
                    launch([index], held)

    half = sums.shape[1] // tiles
    chunk = half // crew
    rank = shard // mates

    def settle(phase, piece, ref):
        spot = phase * PIECES + piece
        pltpu.make_async_copy(ref, ref, sum_send.at[spot]).wait()
        pltpu.make_async_copy(ref, ref, sum_recv.at[spot]).wait()

    def pass_on(phase, piece, src, dst, peer):
        spot = phase * PIECES + piece
        remote(src, dst, sum_send.at[spot], sum_recv.at[spot], peer).start()

    mine = at(tile * half, half)
    own = at(tile * half + rank * chunk, chunk)

    for piece in range(PIECES):
        each(
            tiles,
            lambda step, piece=piece: pass_on(
                0,
                piece,
                sums.at[piece, at(lax.rem(tile + step, tiles) * half, half)],
                pair_in.at[piece, step - 1],
                tile_peer(step),
            ),
        )
    launch(rim_moves)
    send_acts(2)

    def out_forward(frame):
        joined = jnp.concatenate([flat(acts[frame + REACH - lag]) for lag in range(TAPS)], axis=1)
        value = flat(cells[frame, pl.ds(1, height)]).astype(jnp.float32)
        value = value + jnp.dot(joined, time_ref[...], preferred_element_type=jnp.float32)
        out_f[frame] = value.astype(KIND).reshape(height, width, channels)

    def out_reverse(frame):
        joined = jnp.concatenate([flat(acts[frame + REACH + lag]) for lag in range(TAPS)], axis=1)
        value = flat(cells[frame, pl.ds(1, height)]).astype(jnp.float32)
        value = value + jnp.dot(joined, time_ref[...], preferred_element_type=jnp.float32)
        out_r[frame] = value.astype(KIND).reshape(height, width, channels)

    def outputs(reach):
        for frame in range(count):
            if max(0, REACH - frame) == reach:
                out_forward(frame)
            if max(0, REACH - (count - 1 - frame)) == reach:
                out_reverse(frame)

    outputs(0)

    def scatter(piece):
        settle(0, piece, pair_in.at[piece])
        if piece == 0:
            send_acts(3)
        value = sums[piece, mine, :]
        for index in range(tiles - 1):
            value = value + pair_in[piece, index]
        mid[piece] = value
        mid_out[piece] = value.astype(KIND)
        each(
            crew,
            lambda step: pass_on(
                1,
                piece,
                mid_out.at[piece, at(lax.rem(rank + step, crew) * chunk, chunk)],
                shard_in.at[piece, step - 1],
                crew_peer(step),
            ),
        )

    for piece in range(PIECES):
        scatter(piece)
    send_acts(4)

    arrive(rim_moves)
    edge = columns(count * width, width, channels)
    for side, row in ((0, 0), (1, height + 1)):
        rim = spread(flat(rim_in[side]).astype(jnp.float32), edge, width)
        wide[:, row] = rim.reshape(count, width, TAPS * channels)

    def input_grads(frame):
        joined = jnp.concatenate(
            [flat(wide[frame, pl.ds(2 - row, height)]) for row in range(TAPS)], axis=1
        )
        value = flat(cot_f[frame]).astype(jnp.float32) + flat(cot_r[frame + REACH]).astype(jnp.float32)
        value = value + across(joined, space_back[...])
        grad_in[frame] = value.astype(KIND).reshape(height, width, channels)

    frames(0, count, input_grads)
    send_acts(5)

    def share_mates(piece):
        settle(1, piece, shard_in.at[piece])
        value = lax.fori_loop(
            0,
            crew - 1,
            lambda index, value: value + shard_in[piece, index].astype(jnp.float32),
            mid[piece, at(rank * chunk, chunk), :],
        )
        mate_out[piece] = value
        if mates == 2:
            pass_on(
                2,
                piece,
                mate_out.at[piece],
                mate_in.at[piece],
                {"tm": shard + 1 - 2 * lax.rem(shard, 2)},
            )

    for piece in range(PIECES):
        share_mates(piece)
    send_acts(6)

    def gather(piece):
        value = mate_out[piece]
        if mates == 2:
            settle(2, piece, mate_in.at[piece])
            value = value + mate_in[piece]
        total[piece, own, :] = (value * scale).astype(KIND)
        each(
            crew,
            lambda step: pass_on(
                3, piece, total.at[piece, own], total.at[piece, own], crew_peer(step)
            ),
        )

    for piece in range(PIECES):
        gather(piece)
    send_acts(7)

    arrive(act_moves[0])
    outputs(1)

    def forward_piece(piece):
        settle(3, piece, total.at[piece, pl.ds(0, (crew - 1) * chunk)])
        each(
            tiles,
            lambda step: pass_on(
                4, piece, total.at[piece, mine], total.at[piece, mine], tile_peer(step)
            ),
        )

    for piece in range(PIECES):
        forward_piece(piece)
    for reach in range(1, REACH):
        arrive(act_moves[reach])
        outputs(reach + 1)
    for piece in range(PIECES):
        settle(4, piece, total.at[piece, pl.ds(0, (tiles - 1) * half)])
    for tap in range(4 * TAPS):
        value = total[tap // (4 * TAPS // PIECES), block(tap % (4 * TAPS // PIECES)), :].astype(jnp.float32)
        if tap < TAPS:
            grad_t[block(tap), :] = value
        else:
            grad_s[block(tap - TAPS), :] = value
    leave(range(len(moves)))


def deliver_kernel(*refs):
    count = (len(refs) - 1) // 2
    stores = [
        pltpu.make_async_copy(refs[index], refs[count + index], refs[-1].at[index])
        for index in range(count)
    ]
    for store in stores:
        store.start()
    for store in stores:
        store.wait()


def deliver(*values):
    hbm = pl.BlockSpec(memory_space=pl.ANY)
    vmem = pl.BlockSpec(memory_space=pltpu.VMEM)
    count = len(values)
    return pl.pallas_call(
        deliver_kernel,
        out_shape=tuple(jax.ShapeDtypeStruct(value.shape, value.dtype) for value in values),
        in_specs=[vmem] * count,
        out_specs=(hbm,) * count,
        scratch_shapes=[pltpu.SemaphoreType.DMA((count,))],
        compiler_params=pltpu.CompilerParams(vmem_limit_bytes=VMEM_LIMIT),
    )(*(pltpu.with_memory_space_constraint(value, pltpu.VMEM) for value in values))


def body(latent, cot_forward, cot_reverse, spatial_weight, temporal_weight):
    tiles, shards = lax.axis_size("tile"), lax.axis_size("tm")
    count, height, width, channels = latent.shape
    positions = count * height * width * shards * tiles
    scale = 1.0 / math.sqrt(positions)
    mates = MATES if shards % MATES == 0 else 1
    crew = shards // mates
    rows = 4 * TAPS * channels // PIECES
    unit = 16 * tiles * crew
    padded = -(-rows // unit) * unit
    half = padded // tiles
    chunk = half // crew
    stages = max(1, (shards - 2).bit_length())
    parts = PARTS if height % PARTS == 0 else 1
    moves = 4 + REACH * 2 + REACH * 2 * parts
    vmem = pl.BlockSpec(memory_space=pltpu.VMEM)
    hbm = pl.BlockSpec(memory_space=pltpu.HBM)
    results = pl.pallas_call(
        functools.partial(kernel, tiles, shards, scale),
        out_shape=(
            pltpu.VMEM(latent.shape, KIND),
            pltpu.VMEM(latent.shape, KIND),
            pltpu.VMEM(latent.shape, KIND),
            pltpu.VMEM((9 * channels, channels), jnp.float32),
            pltpu.VMEM((3 * channels, channels), jnp.float32),
        ),
        in_specs=[hbm] * 5,
        out_specs=(vmem,) * 5,
        scratch_shapes=[
            pltpu.VMEM((count, height + 2, width, channels), KIND),
            pltpu.VMEM((count + REACH, height, width, channels), KIND),
            pltpu.VMEM((count + REACH, height, width, channels), KIND),
            pltpu.VMEM((count + 2 * REACH, height, width, channels), KIND),
            pltpu.VMEM((count, height * width, channels), jnp.float32),
            pltpu.VMEM((count, height * width, channels), jnp.float32),
            pltpu.VMEM((count, height + 2, width, TAPS * channels), KIND),
            pltpu.VMEM((2, count, width, channels), KIND),
            pltpu.VMEM((2, count, width, channels), KIND),
            pltpu.VMEM((9 * channels, channels), KIND),
            pltpu.VMEM((3 * channels, channels), KIND),
            pltpu.VMEM((3 * channels, 3 * channels), KIND),
            pltpu.VMEM((channels, 9 * channels), KIND),
            pltpu.VMEM((channels, 6 * channels), KIND),
            pltpu.VMEM((PIECES, padded, channels), jnp.float32),
            pltpu.VMEM((PIECES, tiles - 1, half, channels), jnp.float32),
            pltpu.VMEM((PIECES, half, channels), jnp.float32),
            pltpu.VMEM((PIECES, half, channels), KIND),
            pltpu.VMEM((PIECES, crew - 1, chunk, channels), KIND),
            pltpu.VMEM((PIECES, chunk, channels), jnp.float32),
            pltpu.VMEM((PIECES, chunk, channels), jnp.float32),
            pltpu.VMEM((PIECES, padded, channels), KIND),
            pltpu.SemaphoreType.DMA((5,)),
            pltpu.SemaphoreType.REGULAR((stages,)),
            pltpu.SemaphoreType.DMA((moves,)),
            pltpu.SemaphoreType.DMA((moves,)),
            pltpu.SemaphoreType.DMA((5 * PIECES,)),
            pltpu.SemaphoreType.DMA((5 * PIECES,)),
        ],
        compiler_params=pltpu.CompilerParams(
            collective_id=0, has_side_effects=True, vmem_limit_bytes=VMEM_LIMIT
        ),
    )(
        *(
            pltpu.with_memory_space_constraint(value, pltpu.HBM)
            for value in (
                latent,
                cot_forward,
                cot_reverse,
                spatial_weight.reshape(9 * channels, channels),
                temporal_weight.reshape(3 * channels, channels),
            )
        ),
    )
    out_f, out_r, grad_in, grad_s, grad_t = deliver(*results)
    return (
        out_f,
        out_r,
        grad_in,
        grad_s.reshape(spatial_weight.shape),
        grad_t.reshape(temporal_weight.shape),
    )


def solution(mesh):
    split, copied = P("tm", "tile", None, None), P()
    return jax.shard_map(
        body,
        mesh=mesh,
        in_specs=(split, split, split, copied, copied),
        out_specs=(split, split, split, copied, copied),
        check_vma=False,
    )
```

```python
import functools
import math

import jax
import jax.numpy as jnp
from jax import lax
from jax.experimental import pallas as pl
from jax.experimental.pallas import tpu as pltpu
from jax.sharding import PartitionSpec as P

MESH = pl.DeviceIdType.MESH
KIND = jnp.bfloat16
TAPS = 3
REACH = TAPS - 1
PIECES = 2
PARTS = 4
MATES = 2
HOLD = 1
TURN = False
SLABS = 1
ACTS_INNER = (0,4,4,4,8,8,12,16)
ACTS_SIDE = (0, 0, 4, 4, 8, 8, 12, 16)
ACTS_INNER_ODD = (0,0,0,4,8,8,12,16)
ACTS_SIDE_ODD = (0, 0, 4, 4, 8, 8, 12, 16)
ACTS_FAR_ODD = (0, 0, 4, 4, 8, 8, 12, 16)
ACTS_FAR = (0, 0, 4, 4, 8, 8, 12, 16)
VMEM_LIMIT = 32 << 20


def at(start, size):
    return pl.ds(pl.multiple_of(start, 16), size)


def each(count, act):
    def step(index, carry):
        act(index)
        return carry

    lax.fori_loop(1, count, step, 0)


def frames(first, last, act):
    def step(index, carry):
        act(index)
        return carry

    lax.fori_loop(first, last, step, 0)


def columns(rows, width, channels):
    place = lax.broadcasted_iota(jnp.int32, (rows // width, width, channels), 1)
    return place.reshape(rows, channels)


def before(value, place):
    return jnp.where(place == 0, 0.0, pltpu.roll(value, 1, 0))


def after(value, place, width):
    return jnp.where(place == width - 1, 0.0, pltpu.roll(value, value.shape[0] - 1, 0))


def spread(value, place, width):
    return jnp.concatenate(
        [after(value, place, width).astype(KIND), value.astype(KIND), before(value, place).astype(KIND)],
        axis=1,
    )


def flat(value):
    return value.reshape(-1, value.shape[-1])


def across(left, right):
    return lax.dot_general(
        left, right, (((1,), (1,)), ((), ())), preferred_element_type=jnp.float32
    )


def over(left, right):
    return jnp.dot(left, right, preferred_element_type=jnp.float32)


def contract(left, right):
    return lax.dot_general(
        left, right, (((0,), (0,)), ((), ())), preferred_element_type=jnp.float32
    )


def kernel(
    tiles,
    shards,
    scale,
    latent_ref,
    fwd_ref,
    rev_ref,
    space_hbm,
    time_hbm,
    out_f,
    out_r,
    grad_in,
    grad_s,
    grad_t,
    cells,
    cot_f,
    cot_r,
    acts,
    gates,
    pulls,
    tilted,
    wide,
    rim_out,
    rim_in,
    space_ref,
    time_ref,
    space_fwd,
    space_back,
    time_back,
    sums,
    pair_in,
    mid,
    mid_out,
    shard_in,
    mate_out,
    mate_in,
    total,
    load_sem,
    ready,
    clear,
    halo_send,
    halo_recv,
    sum_send,
    sum_recv,
):
    tile, shard = lax.axis_index("tile"), lax.axis_index("tm")
    count, height, width, channels = latent_ref.shape
    plane = height * width
    mates = MATES if shards % MATES == 0 else 1
    crew = shards // mates

    def tile_peer(step):
        return {"tile": lax.rem(tile + step, tiles)}

    def shard_peer(step):
        return {"tm": lax.rem(shard + step, shards)}

    def crew_peer(step):
        return {"tm": lax.rem(shard + step * mates, shards)}

    def signal(semaphore, peer):
        pl.semaphore_signal(semaphore, inc=1, device_id=peer, device_id_type=MESH)

    loads = [
        pltpu.make_async_copy(src, dst, load_sem.at[index])
        for index, (src, dst) in enumerate(
            (
                (space_hbm, space_ref),
                (time_hbm, time_ref),
                (latent_ref, cells.at[:, pl.ds(1, height)]),
                (fwd_ref, cot_f.at[pl.ds(0, count)]),
                (rev_ref, cot_r.at[pl.ds(REACH, count)]),
            )
        )
    ]
    barrier = pltpu.get_barrier_semaphore()
    has_next_tile, has_last_tile = tile < tiles - 1, tile > 0
    has_next_shard, has_last_shard = shard < shards - 1, shard > 0

    def around(semaphore, span):
        pl.when(shard + span < shards)(lambda: signal(semaphore, {"tm": shard + span}))
        pl.when(shard >= span)(lambda: signal(semaphore, {"tm": shard - span}))

    def near(span):
        return (shard + span < shards).astype(jnp.int32) + (shard >= span).astype(jnp.int32)

    around(barrier, 1)
    each(tiles, lambda step: signal(barrier, tile_peer(step)))
    for load in loads:
        load.start()

    next_tile, last_tile = tile_peer(1), tile_peer(tiles - 1)
    next_shard, last_shard = shard_peer(1), shard_peer(shards - 1)
    up = (next_tile, has_next_tile, has_last_tile)
    down = (last_tile, has_last_tile, has_next_tile)
    later = (next_shard, has_next_shard, has_last_shard)
    earlier = (last_shard, has_last_shard, has_next_shard)
    moves = []

    def move(src, dst, way):
        moves.append((src, dst, *way))
        return len(moves) - 1

    cell_moves = [
        move(latent_ref.at[:, height - 1], cells.at[:, 0], up),
        move(latent_ref.at[:, 0], cells.at[:, height + 1], down),
    ]
    cot_moves = []
    for reach in range(REACH):
        cot_moves.append(
            [
                move(fwd_ref.at[reach], cot_f.at[count + reach], earlier),
                move(rev_ref.at[count - 1 - reach], cot_r.at[REACH - 1 - reach], later),
            ]
        )
    rim_moves = [move(rim_out.at[1], rim_in.at[0], up), move(rim_out.at[0], rim_in.at[1], down)]
    parts = PARTS if height % PARTS == 0 else 1
    rows = height // parts
    act_moves = []
    for reach in range(REACH):
        group = []
        for part in range(parts):
            cut = pl.ds(part * rows, rows)
            group.append(
                move(acts.at[count + 1 - reach, cut], acts.at[1 - reach, cut], later)
            )
            group.append(
                move(acts.at[REACH + reach, cut], acts.at[count + REACH + reach, cut], earlier)
            )
        act_moves.append(group)

    def remote(src, dst, send, recv, peer):
        return pltpu.make_async_remote_copy(
            src_ref=src, dst_ref=dst, send_sem=send, recv_sem=recv, device_id=peer, device_id_type=MESH
        )

    copies = [
        remote(src, dst, halo_send.at[index], halo_recv.at[index], peer)
        for index, (src, dst, peer, _, _) in enumerate(moves)
    ]

    def launch(indices, only=None):
        for index in indices:
            ready_to = moves[index][3]
            if only is not None:
                ready_to = jnp.logical_and(ready_to, only)
            pl.when(ready_to)(copies[index].start)

    def arrive(indices):
        for index in indices:
            pl.when(moves[index][4])(copies[index].wait_recv)

    def leave(indices):
        for index in indices:
            pl.when(moves[index][3])(copies[index].wait_send)

    pl.semaphore_wait(barrier, tiles - 1 + near(1))
    corner = (lax.rem(shard, 4) == 0, lax.rem(shard, 4) == 3)
    launch(cell_moves)
    launch(cot_moves[0])
    for group in cot_moves[1:]:
        for index, held in zip(group, corner):
            launch([index], jnp.logical_not(held) if HOLD else None)
    spans = []
    span = 1
    while span < shards - 1:
        spans.append(span)
        span *= 2

    def tell(index):
        around(ready.at[index], spans[index])

    def hear(index):
        pl.semaphore_wait(ready.at[index], near(spans[index]))

    tell(0)
    for index in range(len(moves)):
        target = moves[index][1]

        @pl.when(jnp.logical_not(moves[index][4]))
        def _(target=target):
            target[...] = jnp.zeros(target.shape, target.dtype)

    sums[...] = jnp.zeros_like(sums)
    place = columns(plane, width, channels)
    loads[0].wait()
    loads[1].wait()

    def block(index):
        return slice(index * channels, (index + 1) * channels)

    for row in range(TAPS):
        weight = time_ref[block(row), :]
        time_back[:, block(REACH - row)] = weight
        time_back[:, block(TAPS + row)] = weight
        for col in range(TAPS):
            weight = space_ref[block(row * TAPS + col), :]
            space_fwd[block(row), block(col)] = weight
            space_back[:, block(row * TAPS + col)] = weight

    def window(frame):
        return jnp.concatenate(
            [flat(cells[frame, pl.ds(row, height)]) for row in range(TAPS)], axis=1
        )

    loads[2].wait()
    arrive(cell_moves)

    def convolve(frame):
        taken = jnp.dot(window(frame), space_fwd[...], preferred_element_type=jnp.float32)
        value = (
            before(taken[:, :channels], place)
            + taken[:, channels : 2 * channels]
            + after(taken[:, 2 * channels :], place, width)
        )
        share = 1.0 / (1.0 + jnp.exp(-value))
        gates[frame] = share * (1.0 + value * (1.0 - share))
        act = value * share
        acts[frame + REACH] = act.astype(KIND).reshape(height, width, channels)

    frames(0, count, convolve)
    hear(0)
    for index in range(1, len(spans)):
        if index == 1:
            tell(1)
    inner = lax.rem(shard + shard // 2, 2) == 1
    outer = jnp.logical_not(inner)
    even = lax.rem(tile, 2) == 0
    odd = jnp.logical_not(even)
    early = jnp.logical_and(inner, even)
    act_ways = ([group[0::2] for group in act_moves], [group[1::2] for group in act_moves])

    def send_acts(moment):
        before = max(0, moment - 1)
        for groups, far in zip(act_ways, (corner[1], corner[0])):
            order = [index for group in groups for index in group]
            side = jnp.logical_and(outer, jnp.logical_not(far))
            both = jnp.logical_and
            for kind, table in (
                (both(inner, even), ACTS_INNER),
                (both(inner, odd), ACTS_INNER_ODD),
                (both(side, even), ACTS_SIDE),
                (both(side, odd), ACTS_SIDE_ODD),
                (both(far, even), ACTS_FAR),
                (both(far, odd), ACTS_FAR_ODD),
            ):
                first = table[before] * len(order) // 16 if moment else 0
                last = table[moment] * len(order) // 16
                if last > first:
                    launch(order[first:last], kind)

    send_acts(0)

    def add_lag(lag, value):
        sums[0, block(lag), :] += value

    def stage_of(frame):
        return max(0, REACH - frame, REACH - (count - 1 - frame))

    def own_pull(frame):
        low = max(0, frame + REACH - (count - 1))
        high = min(REACH, frame)
        fwd = [flat(cot_f[frame + lag]) for lag in range(REACH - low, -1, -1)]
        rev = [flat(cot_r[frame + REACH - lag]) for lag in range(high + 1)]
        joined = jnp.concatenate(fwd + rev, axis=1)
        columns_of = slice(low * channels, (TAPS + high + 1) * channels)
        pulls[frame] = across(joined, time_back[:, columns_of])
        lags = contract(flat(acts[frame + REACH]), joined)
        for index in range(len(fwd)):
            add_lag(REACH - low - index, lags[:, block(index)])
        for lag in range(high + 1):
            add_lag(lag, lags[:, block(len(fwd) + lag)])

    loads[3].wait()
    loads[4].wait()
    for frame in range(count):
        own_pull(frame)
        if stage_of(frame) == REACH:
            spot = slice(min(frame, 1) * plane, (min(frame, 1) + 1) * plane)
            tilted[: TAPS * channels, spot] = window(frame).T
            tilted[TAPS * channels :, spot] = flat(acts[frame + REACH]).T
    for index in range(1, len(spans)):
        hear(index)
        if index + 1 < len(spans):
            tell(index + 1)

    def halo_terms(frame, reach):
        terms = []
        lag = frame + reach
        if lag <= REACH:
            terms.append((lag, cot_r, REACH - reach))
        lag = count - 1 - frame + reach
        if lag <= REACH:
            terms.append((lag, cot_f, count + reach - 1))
        return terms

    def pull_halo(frame, reach):
        pull = pulls[frame]
        for lag, source, index in halo_terms(frame, reach):
            taken = flat(source[index])
            pull = pull + across(taken, time_back[:, block(TAPS + lag)])
        return pull

    def lag_halo(frame, reach):
        for lag, source, index in halo_terms(frame, reach):
            add_lag(lag, contract(flat(acts[frame + REACH]), flat(source[index])))

    def shift_frame(frame, pull):
        grad = (pull * gates[frame]).astype(KIND)
        shifted = spread(grad.astype(jnp.float32), place, width)
        wide[frame, pl.ds(1, height)] = shifted.reshape(height, width, TAPS * channels)
        rim_out[0, frame] = grad[:width]
        rim_out[1, frame] = grad[plane - width :]
        return shifted

    def add_taps(part):
        for row in range(TAPS):
            for col in range(TAPS):
                tap = TAPS + row * TAPS + col
                spot = block(tap % (4 * TAPS // PIECES))
                sums[tap // (4 * TAPS // PIECES), spot, :] += part[block(row), block(col)]

    def settle_frame(frame, pull):
        add_taps(contract(window(frame), shift_frame(frame, pull)))

    ends = [frame for frame in range(count) if stage_of(frame) == REACH]

    def settle_ends():
        shifted = [shift_frame(frame, pull_halo(frame, REACH)) for frame in ends]
        halos = []
        for frame in ends:
            terms = halo_terms(frame, REACH)
            assert len(terms) == 1 and terms[0][0] == REACH
            halos.append(flat(terms[0][1][terms[0][2]]))
        add_lag(REACH, over(tilted[TAPS * channels :, :], jnp.concatenate(halos, axis=0)))
        add_taps(over(tilted[: TAPS * channels, :], jnp.concatenate(shifted, axis=0)))

    for frame in range(count):
        if stage_of(frame) == 0:
            settle_frame(frame, pulls[frame])
    cot_all = [index for group in cot_moves for index in group]

    def drain():
        leave(cot_all)
        each(tiles, lambda step: signal(clear, tile_peer(step)))

    def await_clear():
        pl.semaphore_wait(clear, tiles - 1)

    for reach in range(1, REACH + 1):
        if reach == REACH:
            pl.when(inner)(drain)
            pl.when(early)(await_clear)
            send_acts(1)
        arrive(cot_moves[reach - 1])
        if reach == 1 and HOLD == 1:
            for group in cot_moves[1:]:
                for index, held in zip(group, corner):
                    launch([index], held)
        if reach == REACH:
            settle_ends()
            break
        for frame in range(count):
            if stage_of(frame) >= reach:
                pull = pull_halo(frame, reach)
                if stage_of(frame) == reach:
                    settle_frame(frame, pull)
                else:
                    pulls[frame] = pull
                lag_halo(frame, reach)
        if reach == 1 and HOLD == 2:
            for group in cot_moves[1:]:
                for index, held in zip(group, corner):
                    launch([index], held)

    half = sums.shape[1] // tiles
    chunk = half // crew
    rank = shard // mates

    def chunk_of(seat):
        if TURN and mates == 2 and crew % 4 == 0:
            return seat + lax.rem(shard, 2) * (2 - 4 * lax.rem(seat // 2, 2))
        return seat

    seat = chunk_of(rank)
    mate_rank = rank
    if TURN and mates == 2 and crew % 4 == 0:
        mate_rank = rank + 2 - 4 * lax.rem(rank // 2, 2)

    def settle(phase, piece, ref):
        spot = phase * PIECES + piece
        pltpu.make_async_copy(ref, ref, sum_send.at[spot]).wait()
        pltpu.make_async_copy(ref, ref, sum_recv.at[spot]).wait()

    def pass_on(phase, piece, src, dst, peer):
        spot = phase * PIECES + piece
        remote(src, dst, sum_send.at[spot], sum_recv.at[spot], peer).start()

    mine = at(tile * half, half)
    own = at(tile * half + seat * chunk, chunk)

    for piece in range(PIECES):
        each(
            tiles,
            lambda step, piece=piece: pass_on(
                0,
                piece,
                sums.at[piece, at(lax.rem(tile + step, tiles) * half, half)],
                pair_in.at[piece, step - 1],
                tile_peer(step),
            ),
        )
    launch(rim_moves)
    send_acts(2)

    def out_sum(value, frame, turn, lags):
        joined = jnp.concatenate(
            [flat(acts[frame + REACH + turn * lag]) for lag in lags], axis=1
        )
        weight = time_ref[lags[0] * channels : (lags[-1] + 1) * channels, :]
        return value + jnp.dot(joined, weight, preferred_element_type=jnp.float32)

    def out_base(frame):
        return flat(cells[frame, pl.ds(1, height)]).astype(jnp.float32)

    streams = ((out_f, -1, lambda frame: frame), (out_r, 1, lambda frame: count - 1 - frame))

    def outputs(reach):
        for slot, (ref, turn, depth) in enumerate(streams):
            for frame in range(count):
                need = max(0, REACH - depth(frame))
                if need == REACH and reach == REACH - 1:
                    pulls[slot] = out_sum(out_base(frame), frame, turn, range(REACH))
                if need != reach:
                    continue
                if reach == REACH:
                    value = out_sum(pulls[slot], frame, turn, range(REACH, TAPS))
                else:
                    value = out_sum(out_base(frame), frame, turn, range(TAPS))
                ref[frame] = value.astype(KIND).reshape(height, width, channels)

    outputs(0)

    def scatter(piece):
        settle(0, piece, pair_in.at[piece])
        value = sums[piece, mine, :]
        for index in range(tiles - 1):
            value = value + pair_in[piece, index]
        mid[piece] = value
        mid_out[piece] = value.astype(KIND)
        each(
            crew,
            lambda step: pass_on(
                1,
                piece,
                mid_out.at[piece, at(chunk_of(lax.rem(rank + step, crew)) * chunk, chunk)],
                shard_in.at[piece, step - 1],
                crew_peer(step),
            ),
        )

    pl.when(outer)(drain)
    pl.when(jnp.logical_not(early))(await_clear)
    send_acts(3)
    for piece in range(PIECES):
        scatter(piece)
    send_acts(4)

    arrive(rim_moves)
    edge = columns(count * width, width, channels)
    for side, row in ((0, 0), (1, height + 1)):
        rim = spread(flat(rim_in[side]).astype(jnp.float32), edge, width)
        wide[:, row] = rim.reshape(count, width, TAPS * channels)

    def input_grads(frame):
        joined = jnp.concatenate(
            [flat(wide[frame, pl.ds(2 - row, height)]) for row in range(TAPS)], axis=1
        )
        value = flat(cot_f[frame]).astype(jnp.float32) + flat(cot_r[frame + REACH]).astype(jnp.float32)
        value = value + across(joined, space_back[...])
        grad_in[frame] = value.astype(KIND).reshape(height, width, channels)

    frames(0, count, input_grads)
    send_acts(5)

    def share_mates(piece):
        settle(1, piece, shard_in.at[piece])
        value = lax.fori_loop(
            0,
            crew - 1,
            lambda index, value: value + shard_in[piece, index].astype(jnp.float32),
            mid[piece, at(seat * chunk, chunk), :],
        )
        mate_out[piece] = value
        if mates == 2:
            pass_on(
                2,
                piece,
                mate_out.at[piece],
                mate_in.at[piece],
                {"tm": 2 * mate_rank + 1 - lax.rem(shard, 2)},
            )

    for piece in range(PIECES):
        share_mates(piece)
    send_acts(6)

    def gather(piece):
        value = mate_out[piece]
        if mates == 2:
            settle(2, piece, mate_in.at[piece])
            value = value + mate_in[piece]
        total[piece, own, :] = (value * scale).astype(KIND)
        each(
            crew,
            lambda step: pass_on(
                3, piece, total.at[piece, own], total.at[piece, own], crew_peer(step)
            ),
        )

    for piece in range(PIECES):
        gather(piece)
    send_acts(7)

    arrive(act_moves[0])
    outputs(1)

    def forward_piece(piece):
        settle(3, piece, total.at[piece, pl.ds(0, (crew - 1) * chunk)])
        each(
            tiles,
            lambda step: pass_on(
                4, piece, total.at[piece, mine], total.at[piece, mine], tile_peer(step)
            ),
        )

    for piece in range(PIECES):
        forward_piece(piece)
    for reach in range(1, REACH):
        arrive(act_moves[reach])
        outputs(reach + 1)
    for piece in range(PIECES):
        settle(4, piece, total.at[piece, pl.ds(0, (tiles - 1) * half)])
    for tap in range(4 * TAPS):
        value = total[tap // (4 * TAPS // PIECES), block(tap % (4 * TAPS // PIECES)), :].astype(jnp.float32)
        if tap < TAPS:
            grad_t[block(tap), :] = value
        else:
            grad_s[block(tap - TAPS), :] = value
    leave([index for index in range(len(moves)) if index not in cot_all])


def deliver_kernel(*refs):
    count = (len(refs) - 1) // 2
    stores = []
    for index in range(count):
        source, target = refs[index], refs[count + index]
        cuts = SLABS if source.shape[0] % SLABS == 0 else 1
        size = source.shape[0] // cuts
        for cut in range(cuts):
            rows = pl.ds(cut * size, size)
            stores.append(
                pltpu.make_async_copy(source.at[rows], target.at[rows], refs[-1].at[len(stores)])
            )
    for store in stores:
        store.start()
    for store in stores:
        store.wait()


def deliver(*values):
    hbm = pl.BlockSpec(memory_space=pl.ANY)
    vmem = pl.BlockSpec(memory_space=pltpu.VMEM)
    count = len(values)
    return pl.pallas_call(
        deliver_kernel,
        out_shape=tuple(jax.ShapeDtypeStruct(value.shape, value.dtype) for value in values),
        in_specs=[vmem] * count,
        out_specs=(hbm,) * count,
        scratch_shapes=[pltpu.SemaphoreType.DMA((count * SLABS,))],
        compiler_params=pltpu.CompilerParams(vmem_limit_bytes=VMEM_LIMIT),
    )(*(pltpu.with_memory_space_constraint(value, pltpu.VMEM) for value in values))


def body(latent, cot_forward, cot_reverse, spatial_weight, temporal_weight):
    tiles, shards = lax.axis_size("tile"), lax.axis_size("tm")
    count, height, width, channels = latent.shape
    positions = count * height * width * shards * tiles
    scale = 1.0 / math.sqrt(positions)
    mates = MATES if shards % MATES == 0 else 1
    crew = shards // mates
    rows = 4 * TAPS * channels // PIECES
    unit = 16 * tiles * crew
    padded = -(-rows // unit) * unit
    half = padded // tiles
    chunk = half // crew
    stages = max(1, (shards - 2).bit_length())
    parts = PARTS if height % PARTS == 0 else 1
    moves = 4 + REACH * 2 + REACH * 2 * parts
    vmem = pl.BlockSpec(memory_space=pltpu.VMEM)
    hbm = pl.BlockSpec(memory_space=pltpu.HBM)
    results = pl.pallas_call(
        functools.partial(kernel, tiles, shards, scale),
        out_shape=(
            pltpu.VMEM(latent.shape, KIND),
            pltpu.VMEM(latent.shape, KIND),
            pltpu.VMEM(latent.shape, KIND),
            pltpu.VMEM((9 * channels, channels), jnp.float32),
            pltpu.VMEM((3 * channels, channels), jnp.float32),
        ),
        in_specs=[hbm] * 5,
        out_specs=(vmem,) * 5,
        scratch_shapes=[
            pltpu.VMEM((count, height + 2, width, channels), KIND),
            pltpu.VMEM((count + REACH, height, width, channels), KIND),
            pltpu.VMEM((count + REACH, height, width, channels), KIND),
            pltpu.VMEM((count + 2 * REACH, height, width, channels), KIND),
            pltpu.VMEM((count, height * width, channels), jnp.float32),
            pltpu.VMEM((count, height * width, channels), jnp.float32),
            pltpu.VMEM(((TAPS + 1) * channels, min(2, count) * height * width), KIND),
            pltpu.VMEM((count, height + 2, width, TAPS * channels), KIND),
            pltpu.VMEM((2, count, width, channels), KIND),
            pltpu.VMEM((2, count, width, channels), KIND),
            pltpu.VMEM((9 * channels, channels), KIND),
            pltpu.VMEM((3 * channels, channels), KIND),
            pltpu.VMEM((3 * channels, 3 * channels), KIND),
            pltpu.VMEM((channels, 9 * channels), KIND),
            pltpu.VMEM((channels, 6 * channels), KIND),
            pltpu.VMEM((PIECES, padded, channels), jnp.float32),
            pltpu.VMEM((PIECES, tiles - 1, half, channels), jnp.float32),
            pltpu.VMEM((PIECES, half, channels), jnp.float32),
            pltpu.VMEM((PIECES, half, channels), KIND),
            pltpu.VMEM((PIECES, crew - 1, chunk, channels), KIND),
            pltpu.VMEM((PIECES, chunk, channels), jnp.float32),
            pltpu.VMEM((PIECES, chunk, channels), jnp.float32),
            pltpu.VMEM((PIECES, padded, channels), KIND),
            pltpu.SemaphoreType.DMA((5,)),
            pltpu.SemaphoreType.REGULAR((stages,)),
            pltpu.SemaphoreType.REGULAR,
            pltpu.SemaphoreType.DMA((moves,)),
            pltpu.SemaphoreType.DMA((moves,)),
            pltpu.SemaphoreType.DMA((5 * PIECES,)),
            pltpu.SemaphoreType.DMA((5 * PIECES,)),
        ],
        compiler_params=pltpu.CompilerParams(
            collective_id=0, has_side_effects=True, vmem_limit_bytes=VMEM_LIMIT
        ),
    )(
        *(
            pltpu.with_memory_space_constraint(value, pltpu.HBM)
            for value in (
                latent,
                cot_forward,
                cot_reverse,
                spatial_weight.reshape(9 * channels, channels),
                temporal_weight.reshape(3 * channels, channels),
            )
        ),
    )
    out_f, out_r, grad_in, grad_s, grad_t = deliver(*results)
    return (
        out_f,
        out_r,
        grad_in,
        grad_s.reshape(spatial_weight.shape),
        grad_t.reshape(temporal_weight.shape),
    )


def solution(mesh):
    split, copied = P("tm", "tile", None, None), P()
    return jax.shard_map(
        body,
        mesh=mesh,
        in_specs=(split, split, split, copied, copied),
        out_specs=(split, split, split, copied, copied),
        check_vma=False,
    )
```

```python
import functools
import math

import jax
import jax.numpy as jnp
from jax import lax
from jax.experimental import pallas as pl
from jax.experimental.pallas import tpu as pltpu
from jax.sharding import PartitionSpec as P

MESH = pl.DeviceIdType.MESH
KIND = jnp.bfloat16
TAPS = 3
REACH = TAPS - 1
PIECES = 2
PARTS = 4
MATES = 2
HOLD = 2
TURN = True
SLABS = 1
ACTS_INNER = (0,4,4,4,10,10,12,16)
ACTS_SIDE = (0, 0, 4, 4, 8, 8, 12, 16)
ACTS_INNER_ODD = (0,0,0,4,10,10,12,16)
ACTS_SIDE_ODD = (0, 0, 4, 4, 8, 8, 12, 16)
ACTS_FAR_ODD = (0, 0, 4, 4, 8, 8, 12, 16)
ACTS_FAR = (0, 0, 4, 4, 8, 8, 12, 16)
VMEM_LIMIT = 32 << 20


def at(start, size):
    return pl.ds(pl.multiple_of(start, 16), size)


def each(count, act):
    def step(index, carry):
        act(index)
        return carry

    lax.fori_loop(1, count, step, 0)


def frames(first, last, act):
    def step(index, carry):
        act(index)
        return carry

    lax.fori_loop(first, last, step, 0)


def columns(rows, width, channels):
    place = lax.broadcasted_iota(jnp.int32, (rows // width, width, channels), 1)
    return place.reshape(rows, channels)


def before(value, place):
    return jnp.where(place == 0, 0.0, pltpu.roll(value, 1, 0))


def after(value, place, width):
    return jnp.where(place == width - 1, 0.0, pltpu.roll(value, value.shape[0] - 1, 0))


def spread(value, place, width):
    return jnp.concatenate(
        [after(value, place, width).astype(KIND), value.astype(KIND), before(value, place).astype(KIND)],
        axis=1,
    )


def flat(value):
    return value.reshape(-1, value.shape[-1])


def across(left, right):
    return lax.dot_general(
        left, right, (((1,), (1,)), ((), ())), preferred_element_type=jnp.float32
    )


def over(left, right):
    return jnp.dot(left, right, preferred_element_type=jnp.float32)


def contract(left, right):
    return lax.dot_general(
        left, right, (((0,), (0,)), ((), ())), preferred_element_type=jnp.float32
    )


def kernel(
    tiles,
    shards,
    scale,
    latent_ref,
    fwd_ref,
    rev_ref,
    space_hbm,
    time_hbm,
    out_f,
    out_r,
    grad_in,
    grad_s,
    grad_t,
    cells,
    cot_f,
    cot_r,
    acts,
    gates,
    pulls,
    tilted,
    wide,
    rim_out,
    rim_in,
    space_ref,
    time_ref,
    space_fwd,
    space_back,
    time_back,
    sums,
    pair_in,
    mid,
    mid_out,
    shard_in,
    mate_out,
    mate_in,
    total,
    load_sem,
    ready,
    clear,
    halo_send,
    halo_recv,
    sum_send,
    sum_recv,
):
    tile, shard = lax.axis_index("tile"), lax.axis_index("tm")
    count, height, width, channels = latent_ref.shape
    plane = height * width
    mates = MATES if shards % MATES == 0 else 1
    crew = shards // mates

    def tile_peer(step):
        return {"tile": lax.rem(tile + step, tiles)}

    def shard_peer(step):
        return {"tm": lax.rem(shard + step, shards)}

    def crew_peer(step):
        return {"tm": lax.rem(shard + step * mates, shards)}

    def signal(semaphore, peer):
        pl.semaphore_signal(semaphore, inc=1, device_id=peer, device_id_type=MESH)

    loads = [
        pltpu.make_async_copy(src, dst, load_sem.at[index])
        for index, (src, dst) in enumerate(
            (
                (space_hbm, space_ref),
                (time_hbm, time_ref),
                (latent_ref, cells.at[:, pl.ds(1, height)]),
                (fwd_ref, cot_f.at[pl.ds(0, count)]),
                (rev_ref, cot_r.at[pl.ds(REACH, count)]),
            )
        )
    ]
    barrier = pltpu.get_barrier_semaphore()
    has_next_tile, has_last_tile = tile < tiles - 1, tile > 0
    has_next_shard, has_last_shard = shard < shards - 1, shard > 0

    def around(semaphore, span):
        pl.when(shard + span < shards)(lambda: signal(semaphore, {"tm": shard + span}))
        pl.when(shard >= span)(lambda: signal(semaphore, {"tm": shard - span}))

    def near(span):
        return (shard + span < shards).astype(jnp.int32) + (shard >= span).astype(jnp.int32)

    around(barrier, 1)
    each(tiles, lambda step: signal(barrier, tile_peer(step)))
    for load in loads:
        load.start()

    next_tile, last_tile = tile_peer(1), tile_peer(tiles - 1)
    next_shard, last_shard = shard_peer(1), shard_peer(shards - 1)
    up = (next_tile, has_next_tile, has_last_tile)
    down = (last_tile, has_last_tile, has_next_tile)
    later = (next_shard, has_next_shard, has_last_shard)
    earlier = (last_shard, has_last_shard, has_next_shard)
    moves = []

    def move(src, dst, way):
        moves.append((src, dst, *way))
        return len(moves) - 1

    cell_moves = [
        move(latent_ref.at[:, height - 1], cells.at[:, 0], up),
        move(latent_ref.at[:, 0], cells.at[:, height + 1], down),
    ]
    cot_moves = []
    for reach in range(REACH):
        cot_moves.append(
            [
                move(fwd_ref.at[reach], cot_f.at[count + reach], earlier),
                move(rev_ref.at[count - 1 - reach], cot_r.at[REACH - 1 - reach], later),
            ]
        )
    rim_moves = [move(rim_out.at[1], rim_in.at[0], up), move(rim_out.at[0], rim_in.at[1], down)]
    parts = PARTS if height % PARTS == 0 else 1
    rows = height // parts
    act_moves = []
    for reach in range(REACH):
        group = []
        for part in range(parts):
            cut = pl.ds(part * rows, rows)
            group.append(
                move(acts.at[count + 1 - reach, cut], acts.at[1 - reach, cut], later)
            )
            group.append(
                move(acts.at[REACH + reach, cut], acts.at[count + REACH + reach, cut], earlier)
            )
        act_moves.append(group)

    def remote(src, dst, send, recv, peer):
        return pltpu.make_async_remote_copy(
            src_ref=src, dst_ref=dst, send_sem=send, recv_sem=recv, device_id=peer, device_id_type=MESH
        )

    copies = [
        remote(src, dst, halo_send.at[index], halo_recv.at[index], peer)
        for index, (src, dst, peer, _, _) in enumerate(moves)
    ]

    def launch(indices, only=None):
        for index in indices:
            ready_to = moves[index][3]
            if only is not None:
                ready_to = jnp.logical_and(ready_to, only)
            pl.when(ready_to)(copies[index].start)

    def arrive(indices):
        for index in indices:
            pl.when(moves[index][4])(copies[index].wait_recv)

    def leave(indices):
        for index in indices:
            pl.when(moves[index][3])(copies[index].wait_send)

    pl.semaphore_wait(barrier, tiles - 1 + near(1))
    corner = (lax.rem(shard, 4) == 0, lax.rem(shard, 4) == 3)
    launch(cell_moves)
    launch(cot_moves[0])
    for group in cot_moves[1:]:
        for index, held in zip(group, corner):
            launch([index], jnp.logical_not(held) if HOLD else None)
    spans = []
    span = 1
    while span < shards - 1:
        spans.append(span)
        span *= 2

    def tell(index):
        around(ready.at[index], spans[index])

    def hear(index):
        pl.semaphore_wait(ready.at[index], near(spans[index]))

    tell(0)
    for index in range(len(moves)):
        target = moves[index][1]

        @pl.when(jnp.logical_not(moves[index][4]))
        def _(target=target):
            target[...] = jnp.zeros(target.shape, target.dtype)

    sums[...] = jnp.zeros_like(sums)
    place = columns(plane, width, channels)
    loads[0].wait()
    loads[1].wait()

    def block(index):
        return slice(index * channels, (index + 1) * channels)

    for row in range(TAPS):
        weight = time_ref[block(row), :]
        time_back[:, block(REACH - row)] = weight
        time_back[:, block(TAPS + row)] = weight
        for col in range(TAPS):
            weight = space_ref[block(row * TAPS + col), :]
            space_fwd[block(row), block(col)] = weight
            space_back[:, block(row * TAPS + col)] = weight

    def window(frame):
        return jnp.concatenate(
            [flat(cells[frame, pl.ds(row, height)]) for row in range(TAPS)], axis=1
        )

    loads[2].wait()
    arrive(cell_moves)

    def convolve(frame):
        taken = jnp.dot(window(frame), space_fwd[...], preferred_element_type=jnp.float32)
        value = (
            before(taken[:, :channels], place)
            + taken[:, channels : 2 * channels]
            + after(taken[:, 2 * channels :], place, width)
        )
        share = 1.0 / (1.0 + jnp.exp(-value))
        gates[frame] = share * (1.0 + value * (1.0 - share))
        act = value * share
        acts[frame + REACH] = act.astype(KIND).reshape(height, width, channels)

    frames(0, count, convolve)
    hear(0)
    for index in range(1, len(spans)):
        if index == 1:
            tell(1)
    inner = lax.rem(shard + shard // 2, 2) == 1
    outer = jnp.logical_not(inner)
    even = lax.rem(tile, 2) == 0
    odd = jnp.logical_not(even)
    early = jnp.logical_and(inner, even)
    act_ways = ([group[0::2] for group in act_moves], [group[1::2] for group in act_moves])

    def send_acts(moment):
        before = max(0, moment - 1)
        for groups, far in zip(act_ways, (corner[1], corner[0])):
            order = [index for group in groups for index in group]
            side = jnp.logical_and(outer, jnp.logical_not(far))
            both = jnp.logical_and
            for kind, table in (
                (both(inner, even), ACTS_INNER),
                (both(inner, odd), ACTS_INNER_ODD),
                (both(side, even), ACTS_SIDE),
                (both(side, odd), ACTS_SIDE_ODD),
                (both(far, even), ACTS_FAR),
                (both(far, odd), ACTS_FAR_ODD),
            ):
                first = table[before] * len(order) // 16 if moment else 0
                last = table[moment] * len(order) // 16
                if last > first:
                    launch(order[first:last], kind)

    send_acts(0)

    def add_lag(lag, value):
        sums[0, block(lag), :] += value

    def stage_of(frame):
        return max(0, REACH - frame, REACH - (count - 1 - frame))

    def own_pull(frame):
        low = max(0, frame + REACH - (count - 1))
        high = min(REACH, frame)
        fwd = [flat(cot_f[frame + lag]) for lag in range(REACH - low, -1, -1)]
        rev = [flat(cot_r[frame + REACH - lag]) for lag in range(high + 1)]
        joined = jnp.concatenate(fwd + rev, axis=1)
        columns_of = slice(low * channels, (TAPS + high + 1) * channels)
        pulls[frame] = across(joined, time_back[:, columns_of])
        lags = contract(flat(acts[frame + REACH]), joined)
        for index in range(len(fwd)):
            add_lag(REACH - low - index, lags[:, block(index)])
        for lag in range(high + 1):
            add_lag(lag, lags[:, block(len(fwd) + lag)])

    loads[3].wait()
    loads[4].wait()
    for frame in range(count):
        own_pull(frame)
        if stage_of(frame) == REACH:
            spot = slice(min(frame, 1) * plane, (min(frame, 1) + 1) * plane)
            tilted[: TAPS * channels, spot] = window(frame).T
            tilted[TAPS * channels :, spot] = flat(acts[frame + REACH]).T
    for index in range(1, len(spans)):
        hear(index)
        if index + 1 < len(spans):
            tell(index + 1)

    def halo_terms(frame, reach):
        terms = []
        lag = frame + reach
        if lag <= REACH:
            terms.append((lag, cot_r, REACH - reach))
        lag = count - 1 - frame + reach
        if lag <= REACH:
            terms.append((lag, cot_f, count + reach - 1))
        return terms

    def pull_halo(frame, reach):
        pull = pulls[frame]
        for lag, source, index in halo_terms(frame, reach):
            taken = flat(source[index])
            pull = pull + across(taken, time_back[:, block(TAPS + lag)])
        return pull

    def lag_halo(frame, reach):
        for lag, source, index in halo_terms(frame, reach):
            add_lag(lag, contract(flat(acts[frame + REACH]), flat(source[index])))

    def shift_frame(frame, pull):
        grad = (pull * gates[frame]).astype(KIND)
        shifted = spread(grad.astype(jnp.float32), place, width)
        wide[frame, pl.ds(1, height)] = shifted.reshape(height, width, TAPS * channels)
        rim_out[0, frame] = grad[:width]
        rim_out[1, frame] = grad[plane - width :]
        return shifted

    def add_taps(part):
        for row in range(TAPS):
            for col in range(TAPS):
                tap = TAPS + row * TAPS + col
                spot = block(tap % (4 * TAPS // PIECES))
                sums[tap // (4 * TAPS // PIECES), spot, :] += part[block(row), block(col)]

    def settle_frame(frame, pull):
        add_taps(contract(window(frame), shift_frame(frame, pull)))

    ends = [frame for frame in range(count) if stage_of(frame) == REACH]

    def settle_ends():
        shifted = [shift_frame(frame, pull_halo(frame, REACH)) for frame in ends]
        halos = []
        for frame in ends:
            terms = halo_terms(frame, REACH)
            assert len(terms) == 1 and terms[0][0] == REACH
            halos.append(flat(terms[0][1][terms[0][2]]))
        add_lag(REACH, over(tilted[TAPS * channels :, :], jnp.concatenate(halos, axis=0)))
        add_taps(over(tilted[: TAPS * channels, :], jnp.concatenate(shifted, axis=0)))

    for frame in range(count):
        if stage_of(frame) == 0:
            settle_frame(frame, pulls[frame])
    cot_all = [index for group in cot_moves for index in group]

    def drain():
        leave(cot_all)
        each(tiles, lambda step: signal(clear, tile_peer(step)))

    def await_clear():
        pl.semaphore_wait(clear, tiles - 1)

    for reach in range(1, REACH + 1):
        if reach == REACH:
            pl.when(inner)(drain)
            pl.when(early)(await_clear)
            send_acts(1)
        arrive(cot_moves[reach - 1])
        if reach == 1 and HOLD == 1:
            for group in cot_moves[1:]:
                for index, held in zip(group, corner):
                    launch([index], held)
        if reach == REACH:
            settle_ends()
            break
        for frame in range(count):
            if stage_of(frame) >= reach:
                pull = pull_halo(frame, reach)
                if stage_of(frame) == reach:
                    settle_frame(frame, pull)
                else:
                    pulls[frame] = pull
                lag_halo(frame, reach)
        if reach == 1 and HOLD == 2:
            for group in cot_moves[1:]:
                for index, held in zip(group, corner):
                    launch([index], held)

    half = sums.shape[1] // tiles
    chunk = half // crew
    rank = shard // mates

    def chunk_of(seat):
        if TURN and mates == 2 and crew % 4 == 0:
            return seat + lax.rem(shard, 2) * (2 - 4 * lax.rem(seat // 2, 2))
        return seat

    seat = chunk_of(rank)
    mate_rank = rank
    if TURN and mates == 2 and crew % 4 == 0:
        mate_rank = rank + 2 - 4 * lax.rem(rank // 2, 2)

    def settle(phase, piece, ref):
        spot = phase * PIECES + piece
        pltpu.make_async_copy(ref, ref, sum_send.at[spot]).wait()
        pltpu.make_async_copy(ref, ref, sum_recv.at[spot]).wait()

    def pass_on(phase, piece, src, dst, peer):
        spot = phase * PIECES + piece
        remote(src, dst, sum_send.at[spot], sum_recv.at[spot], peer).start()

    mine = at(tile * half, half)
    own = at(tile * half + seat * chunk, chunk)

    for piece in range(PIECES):
        each(
            tiles,
            lambda step, piece=piece: pass_on(
                0,
                piece,
                sums.at[piece, at(lax.rem(tile + step, tiles) * half, half)],
                pair_in.at[piece, step - 1],
                tile_peer(step),
            ),
        )
    launch(rim_moves)
    send_acts(2)

    def out_sum(value, frame, turn, lags):
        joined = jnp.concatenate(
            [flat(acts[frame + REACH + turn * lag]) for lag in lags], axis=1
        )
        weight = time_ref[lags[0] * channels : (lags[-1] + 1) * channels, :]
        return value + jnp.dot(joined, weight, preferred_element_type=jnp.float32)

    def out_base(frame):
        return flat(cells[frame, pl.ds(1, height)]).astype(jnp.float32)

    streams = ((out_f, -1, lambda frame: frame), (out_r, 1, lambda frame: count - 1 - frame))

    def outputs(reach):
        for slot, (ref, turn, depth) in enumerate(streams):
            for frame in range(count):
                need = max(0, REACH - depth(frame))
                if need == REACH and reach == REACH - 1:
                    pulls[slot] = out_sum(out_base(frame), frame, turn, range(REACH))
                if need != reach:
                    continue
                if reach == REACH:
                    value = out_sum(pulls[slot], frame, turn, range(REACH, TAPS))
                else:
                    value = out_sum(out_base(frame), frame, turn, range(TAPS))
                ref[frame] = value.astype(KIND).reshape(height, width, channels)

    outputs(0)

    def scatter(piece):
        settle(0, piece, pair_in.at[piece])
        value = sums[piece, mine, :]
        for index in range(tiles - 1):
            value = value + pair_in[piece, index]
        mid[piece] = value
        mid_out[piece] = value.astype(KIND)
        each(
            crew,
            lambda step: pass_on(
                1,
                piece,
                mid_out.at[piece, at(chunk_of(lax.rem(rank + step, crew)) * chunk, chunk)],
                shard_in.at[piece, step - 1],
                crew_peer(step),
            ),
        )

    pl.when(outer)(drain)
    pl.when(jnp.logical_not(early))(await_clear)
    send_acts(3)
    for piece in range(PIECES):
        scatter(piece)
    send_acts(4)

    arrive(rim_moves)
    edge = columns(count * width, width, channels)
    for side, row in ((0, 0), (1, height + 1)):
        rim = spread(flat(rim_in[side]).astype(jnp.float32), edge, width)
        wide[:, row] = rim.reshape(count, width, TAPS * channels)

    def input_grads(frame):
        joined = jnp.concatenate(
            [flat(wide[frame, pl.ds(2 - row, height)]) for row in range(TAPS)], axis=1
        )
        value = flat(cot_f[frame]).astype(jnp.float32) + flat(cot_r[frame + REACH]).astype(jnp.float32)
        value = value + across(joined, space_back[...])
        grad_in[frame] = value.astype(KIND).reshape(height, width, channels)

    frames(0, count, input_grads)
    send_acts(5)

    def share_mates(piece):
        settle(1, piece, shard_in.at[piece])
        value = lax.fori_loop(
            0,
            crew - 1,
            lambda index, value: value + shard_in[piece, index].astype(jnp.float32),
            mid[piece, at(seat * chunk, chunk), :],
        )
        mate_out[piece] = value
        if mates == 2:
            pass_on(
                2,
                piece,
                mate_out.at[piece],
                mate_in.at[piece],
                {"tm": 2 * mate_rank + 1 - lax.rem(shard, 2)},
            )

    for piece in range(PIECES):
        share_mates(piece)
    send_acts(6)

    def gather(piece):
        value = mate_out[piece]
        if mates == 2:
            settle(2, piece, mate_in.at[piece])
            value = value + mate_in[piece]
        total[piece, own, :] = (value * scale).astype(KIND)
        each(
            crew,
            lambda step: pass_on(
                3, piece, total.at[piece, own], total.at[piece, own], crew_peer(step)
            ),
        )

    for piece in range(PIECES):
        gather(piece)
    send_acts(7)

    arrive(act_moves[0])
    outputs(1)

    def forward_piece(piece):
        settle(3, piece, total.at[piece, pl.ds(0, (crew - 1) * chunk)])
        each(
            tiles,
            lambda step: pass_on(
                4, piece, total.at[piece, mine], total.at[piece, mine], tile_peer(step)
            ),
        )

    for piece in range(PIECES):
        forward_piece(piece)
    for reach in range(1, REACH):
        arrive(act_moves[reach])
        outputs(reach + 1)
    for piece in range(PIECES):
        settle(4, piece, total.at[piece, pl.ds(0, (tiles - 1) * half)])
    for tap in range(4 * TAPS):
        value = total[tap // (4 * TAPS // PIECES), block(tap % (4 * TAPS // PIECES)), :].astype(jnp.float32)
        if tap < TAPS:
            grad_t[block(tap), :] = value
        else:
            grad_s[block(tap - TAPS), :] = value
    leave([index for index in range(len(moves)) if index not in cot_all])


def deliver_kernel(*refs):
    count = (len(refs) - 1) // 2
    stores = []
    for index in range(count):
        source, target = refs[index], refs[count + index]
        cuts = SLABS if source.shape[0] % SLABS == 0 else 1
        size = source.shape[0] // cuts
        for cut in range(cuts):
            rows = pl.ds(cut * size, size)
            stores.append(
                pltpu.make_async_copy(source.at[rows], target.at[rows], refs[-1].at[len(stores)])
            )
    for store in stores:
        store.start()
    for store in stores:
        store.wait()


def deliver(*values):
    hbm = pl.BlockSpec(memory_space=pl.ANY)
    vmem = pl.BlockSpec(memory_space=pltpu.VMEM)
    count = len(values)
    return pl.pallas_call(
        deliver_kernel,
        out_shape=tuple(jax.ShapeDtypeStruct(value.shape, value.dtype) for value in values),
        in_specs=[vmem] * count,
        out_specs=(hbm,) * count,
        scratch_shapes=[pltpu.SemaphoreType.DMA((count * SLABS,))],
        compiler_params=pltpu.CompilerParams(vmem_limit_bytes=VMEM_LIMIT),
    )(*(pltpu.with_memory_space_constraint(value, pltpu.VMEM) for value in values))


def body(latent, cot_forward, cot_reverse, spatial_weight, temporal_weight):
    tiles, shards = lax.axis_size("tile"), lax.axis_size("tm")
    count, height, width, channels = latent.shape
    positions = count * height * width * shards * tiles
    scale = 1.0 / math.sqrt(positions)
    mates = MATES if shards % MATES == 0 else 1
    crew = shards // mates
    rows = 4 * TAPS * channels // PIECES
    unit = 16 * tiles * crew
    padded = -(-rows // unit) * unit
    half = padded // tiles
    chunk = half // crew
    stages = max(1, (shards - 2).bit_length())
    parts = PARTS if height % PARTS == 0 else 1
    moves = 4 + REACH * 2 + REACH * 2 * parts
    vmem = pl.BlockSpec(memory_space=pltpu.VMEM)
    hbm = pl.BlockSpec(memory_space=pltpu.HBM)
    results = pl.pallas_call(
        functools.partial(kernel, tiles, shards, scale),
        out_shape=(
            pltpu.VMEM(latent.shape, KIND),
            pltpu.VMEM(latent.shape, KIND),
            pltpu.VMEM(latent.shape, KIND),
            pltpu.VMEM((9 * channels, channels), jnp.float32),
            pltpu.VMEM((3 * channels, channels), jnp.float32),
        ),
        in_specs=[hbm] * 5,
        out_specs=(vmem,) * 5,
        scratch_shapes=[
            pltpu.VMEM((count, height + 2, width, channels), KIND),
            pltpu.VMEM((count + REACH, height, width, channels), KIND),
            pltpu.VMEM((count + REACH, height, width, channels), KIND),
            pltpu.VMEM((count + 2 * REACH, height, width, channels), KIND),
            pltpu.VMEM((count, height * width, channels), jnp.float32),
            pltpu.VMEM((count, height * width, channels), jnp.float32),
            pltpu.VMEM(((TAPS + 1) * channels, min(2, count) * height * width), KIND),
            pltpu.VMEM((count, height + 2, width, TAPS * channels), KIND),
            pltpu.VMEM((2, count, width, channels), KIND),
            pltpu.VMEM((2, count, width, channels), KIND),
            pltpu.VMEM((9 * channels, channels), KIND),
            pltpu.VMEM((3 * channels, channels), KIND),
            pltpu.VMEM((3 * channels, 3 * channels), KIND),
            pltpu.VMEM((channels, 9 * channels), KIND),
            pltpu.VMEM((channels, 6 * channels), KIND),
            pltpu.VMEM((PIECES, padded, channels), jnp.float32),
            pltpu.VMEM((PIECES, tiles - 1, half, channels), jnp.float32),
            pltpu.VMEM((PIECES, half, channels), jnp.float32),
            pltpu.VMEM((PIECES, half, channels), KIND),
            pltpu.VMEM((PIECES, crew - 1, chunk, channels), KIND),
            pltpu.VMEM((PIECES, chunk, channels), jnp.float32),
            pltpu.VMEM((PIECES, chunk, channels), jnp.float32),
            pltpu.VMEM((PIECES, padded, channels), KIND),
            pltpu.SemaphoreType.DMA((5,)),
            pltpu.SemaphoreType.REGULAR((stages,)),
            pltpu.SemaphoreType.REGULAR,
            pltpu.SemaphoreType.DMA((moves,)),
            pltpu.SemaphoreType.DMA((moves,)),
            pltpu.SemaphoreType.DMA((5 * PIECES,)),
            pltpu.SemaphoreType.DMA((5 * PIECES,)),
        ],
        compiler_params=pltpu.CompilerParams(
            collective_id=0, has_side_effects=True, vmem_limit_bytes=VMEM_LIMIT
        ),
    )(
        *(
            pltpu.with_memory_space_constraint(value, pltpu.HBM)
            for value in (
                latent,
                cot_forward,
                cot_reverse,
                spatial_weight.reshape(9 * channels, channels),
                temporal_weight.reshape(3 * channels, channels),
            )
        ),
    )
    out_f, out_r, grad_in, grad_s, grad_t = deliver(*results)
    return (
        out_f,
        out_r,
        grad_in,
        grad_s.reshape(spatial_weight.shape),
        grad_t.reshape(temporal_weight.shape),
    )


def solution(mesh):
    split, copied = P("tm", "tile", None, None), P()
    return jax.shard_map(
        body,
        mesh=mesh,
        in_specs=(split, split, split, copied, copied),
        out_specs=(split, split, split, copied, copied),
        check_vma=False,
    )
```
